256 devices in a mesh: seq: 16 (over x_lo, z), mp: 8 (over y, core), dp: 2 (over x_hi).
Axes of the slice: x: 4 (x_hi: 2, x_lo: 2; x = x_hi * 2 + x_lo), y: 4, z: 8, core: 2. Of those that a mesh axis runs over, the one named last changes fastest.
Arguments:
- residual_in: bfloat16 [12288, 2048], P(('dp', 'seq')), parts along dimension 0, may hold values from -6 to 6
- queries: bfloat16 [12288, 2048], P(('dp', 'seq'), 'mp'), parts along dimension 0, may hold values from -30 to 30
- keys: bfloat16 [12288, 2048], P(('dp', 'seq'), 'mp'), parts along dimension 0, may hold values from -10 to 10
- values: bfloat16 [12288, 2048], P(('dp', 'seq'), 'mp'), parts along dimension 0, may hold values from -6 to 6
- w_out: bfloat16 [2048, 2048], P('mp', 'seq'), may hold values from -0.1875 to 0.1875
- conv_value: bfloat16 [2048, 2048], P('seq', 'mp'), may hold values from -0.125 to 0.125
- conv_gate: bfloat16 [2048, 2048], P('seq', 'mp'), may hold values from -0.125 to 0.125
- depth_kernel: float32 [31, 2048], P(None, 'mp'), may hold values from -2 to 2
- conv_out: bfloat16 [2048, 2048], P('mp', 'seq'), may hold values from -0.25 to 0.25
- ffn_in: bfloat16 [2048, 8192], P('seq', 'mp'), may hold values from -0.125 to 0.125
- ffn_down: bfloat16 [8192, 2048], P('mp', 'seq'), may hold values from -0.1875 to 0.1875
- ffn_mask: int32 [96, 64], P(('dp', 'seq'), 'mp'), parts along dimension 0, may hold values 0 or 1
Outputs:
- block_out: float32 [12288, 2048], P(('dp', 'seq', 'mp')), parts along dimension 0
The draws below stay inside these ranges and needn't reach their ends.
There are 2 independent parts, one for each index of `dp`. The reference program is written for one: setup_inputs(seed, part) draws one part's arguments, and reference() takes and returns one part's arrays. A program takes and returns all parts, laid end to end along the dimension named above; an argument that names none is the same for every part. Nothing has to cross between parts.
All inputs are finite; a program needn't handle non-finite values. No bound on the sum of `ffn_mask` on one device may be relied on, other than what follows from the above.
Results may differ from the reference program's by a relative error of at most 0.017.
Values may be sent and summed in bfloat16 or wider, within the bound.
A program may use at most 128 MiB of HBM per device.

```python
import math
import jax
import jax.numpy as jnp
from jax import lax

HEADS = 16
HEAD_DIM = 128
FF = 8192
KERNEL = 31
TILE = 128
CBLOCK = 128
TOK_DEV = 384
D = 2048
FRAMES = 6144
N_MP = 8


def draw_queries(key, part):
    noise_key = jax.random.fold_in(key, 1)
    result = jnp.clip(1.7320508 * jax.random.normal(noise_key, (FRAMES, D), jnp.float32), -10.0, 10.0)
    return result.astype(jnp.bfloat16)


def draw_keys(key, part):
    noise_key = jax.random.fold_in(key, 2)
    result = jnp.clip(1.7320508 * jax.random.normal(noise_key, (FRAMES, D), jnp.float32), -10.0, 10.0)
    return result.astype(jnp.bfloat16)


def touch_ends(array, stream_key, least, high):
    extent = array.shape
    spot = [jax.random.randint(jax.random.fold_in(stream_key, axis), (), 0, extent[axis]) for axis in range(len(extent))]
    array = array.at[tuple(spot)].set(least)
    longest = extent.index(max(extent))
    spot[longest] = (spot[longest] + 1) % extent[longest]
    return array.at[tuple(spot)].set(high)


def levels(stream_key, shape, cuts, low, largest):
    factor_of, own = 1.0, jax.random.fold_in(stream_key, 6)
    for dim, blocks in cuts:
        steps = jnp.exp(jax.random.uniform(jax.random.fold_in(own, dim), (blocks,), jnp.float32, low / len(cuts), largest / len(cuts)))
        factor_of = factor_of * jnp.repeat(steps, shape[dim] // blocks).reshape([-1 if axis == dim else 1 for axis in range(len(shape))])
    return factor_of


def gaussian(own_key, extent, width, reach, cuts=(), held_as=jnp.bfloat16):
    values = width * jax.random.normal(own_key, extent, jnp.float32)
    if cuts:
        values = values * levels(own_key, extent, cuts, -0.22, 0.18)
    return jnp.clip(values, -reach, reach).astype(held_as)


def setup_inputs(seed: int = 0, part: int = 0) -> dict:
    seeds = jax.random.split(jax.random.key(seed), 13)
    part_keys = jax.random.split(jax.random.fold_in(seeds[12], part), 13)
    return {
        "residual_in": gaussian(part_keys[0], (FRAMES, D), 1.0, 6.0, ((0, 16),)),
        "queries": draw_queries(jax.random.fold_in(jax.random.fold_in(seeds[12], part), 71), part),
        "keys": draw_keys(jax.random.fold_in(jax.random.fold_in(seeds[12], part), 71), part),
        "values": gaussian(part_keys[3], (FRAMES, D), 1.0, 6.0, ((0, 16), (1, 8))),
        "w_out": gaussian(seeds[4], (D, D), (D // 2) ** -0.5, 0.1875, ((0, 8), (1, 16))),
        "conv_value": gaussian(seeds[5], (D, D), D ** -0.5, 0.125, ((0, 16), (1, 8))),
        "conv_gate": gaussian(seeds[6], (D, D), D ** -0.5, 0.125, ((0, 16), (1, 8))),
        "depth_kernel": gaussian(seeds[7], (KERNEL, D), (KERNEL // 4) ** -0.5, 2.0, ((1, 8),), jnp.float32),
        "conv_out": gaussian(seeds[8], (D, D), (D // 4) ** -0.5, 0.25, ((0, 8), (1, 16))),
        "ffn_in": gaussian(seeds[9], (D, FF), D ** -0.5, 0.125, ((0, 16), (1, 8))),
        "ffn_down": gaussian(seeds[10], (FF, D), (FF // 8) ** -0.5, 0.1875, ((0, 8), (1, 16))),
        "ffn_mask": touch_ends((jax.random.randint(part_keys[11], (FRAMES // TILE, FF // CBLOCK), 0, 2) < 1).astype(jnp.int32), jax.random.fold_in(part_keys[11], 1), 0, 1),
    }


def layer_norm(stream):
    row_mean = lax.optimization_barrier(jnp.mean(stream, axis=-1, keepdims=True))
    centered = stream - row_mean
    spread = lax.optimization_barrier(jnp.mean(centered * centered, axis=-1, keepdims=True))
    return centered * lax.rsqrt(spread + 1e-05)

def rounded(product):
    return lax.optimization_barrier(product.astype(jnp.bfloat16)).astype(jnp.float32)

def grouped_sum(left, weight):
    group_width = left.shape[1] // N_MP
    summed = jnp.zeros((left.shape[0], weight.shape[1]), jnp.float32)
    for group in range(N_MP):
        first_col = group * group_width
        product = jnp.dot(left[:, first_col:first_col + group_width], weight[first_col:first_col + group_width], preferred_element_type=jnp.float32)
        summed = summed + rounded(product)
    return summed

def attention(queries, keys, values):
    score_scale = 1.0 / math.sqrt(HEAD_DIM)
    key_heads = keys.astype(jnp.float32).reshape(FRAMES, HEADS, HEAD_DIM)
    value_heads = values.astype(jnp.float32).reshape(FRAMES, HEADS, HEAD_DIM)
    query_blocks = queries.astype(jnp.float32).reshape(FRAMES // TOK_DEV, TOK_DEV, HEADS, HEAD_DIM)

    def one_block(query_heads):
        scores = jnp.einsum('qhd,khd->qhk', query_heads, key_heads) * score_scale
        row_max = lax.optimization_barrier(jnp.max(scores, axis=-1, keepdims=True))
        exp_scores = jnp.exp(scores - row_max)
        row_sum = lax.optimization_barrier(jnp.sum(exp_scores, axis=-1))
        probs = lax.optimization_barrier(exp_scores.astype(jnp.bfloat16)).astype(jnp.float32)
        mixed = jnp.einsum('qhk,khd->qhd', probs, value_heads)
        return (mixed / row_sum[..., None]).astype(jnp.bfloat16)
    return lax.map(one_block, query_blocks).reshape(FRAMES, HEADS * HEAD_DIM)

def reference(residual_in, queries, keys, values, w_out, conv_value, conv_gate, depth_kernel, conv_out, ffn_in, ffn_down, ffn_mask):
    heads_out = attention(queries, keys, values)
    stream_one = residual_in.astype(jnp.float32) + grouped_sum(heads_out, w_out)
    norm_one = layer_norm(stream_one).astype(jnp.bfloat16)
    value_half = jnp.dot(norm_one, conv_value, preferred_element_type=jnp.float32)
    gate_half = jnp.dot(norm_one, conv_gate, preferred_element_type=jnp.float32)
    gated_units = (value_half * jax.nn.sigmoid(gate_half)).astype(jnp.bfloat16)
    half_width = KERNEL // 2
    padded = jnp.pad(gated_units, ((half_width, half_width), (0, 0)))
    depth_out = jnp.zeros((FRAMES, D), jnp.float32)
    for tap_index in range(KERNEL):
        depth_out = depth_out + depth_kernel[tap_index] * padded[tap_index:tap_index + FRAMES].astype(jnp.float32)
    activated = jax.nn.silu(depth_out).astype(jnp.bfloat16)
    stream_two = stream_one + grouped_sum(activated, conv_out)
    norm_two = layer_norm(stream_two).astype(jnp.bfloat16)
    pre_hidden = jnp.dot(norm_two, ffn_in, preferred_element_type=jnp.float32)
    gate_table = jnp.repeat(jnp.repeat(ffn_mask, TILE, axis=0), CBLOCK, axis=1).astype(jnp.float32)
    hidden = (jax.nn.silu(pre_hidden) * gate_table).astype(jnp.bfloat16)
    stream_three = stream_two + 0.5 * grouped_sum(hidden, ffn_down)
    return layer_norm(stream_three)
```

```python
import math

import jax
import jax.numpy as jnp
from jax import lax
from jax.experimental import pallas as pl
from jax.experimental.pallas import tpu as pltpu
from jax.sharding import PartitionSpec as P

MESH = pl.DeviceIdType.MESH
BF, F32 = jnp.bfloat16, jnp.float32
HD = 128
NZ = 8
NY = 4
TOK = 384
ROWS = 48
D = 2048
EPS = 1e-05
TAPS = 31
BQ = 256
RIGHT, LEFT = 0, 1
HOPS_A, HOPS_B = (4, 3), (3, 4)


def layer_norm(x):
    mean = jnp.mean(x, axis=-1, keepdims=True)
    cen = x - mean
    var = jnp.mean(cen * cen, axis=-1, keepdims=True)
    return cen * lax.rsqrt(var + EPS)


def block_kernel(
    res_hbm, q_hbm, k_hbm, v_hbm, wo_hbm, cval_hbm, cgate_hbm, dk_ref, co_hbm, fi_hbm, fd_hbm, mask_ref,
    out_ref,
    qb, kb, vb, m_s, l_s, acc, ob, ho, wo, cv, co, fi, fd, res, stream, ps, xs, xr, rs, rr, nb,
    gp, sh, gs, gr, act, hid, mrow,
    loc, qx_s, qx_r, kv1_s, kv1_r, kv_s, kv_r, wz_s, wz_r, wx_s, wx_r, o_s, o_r,
    pc_s, pc_r, rx_s, rx_r, ag_s, ag_r, agc_s, agc_r, h_s, h_r,
):
    seq, mp, dp = lax.axis_index("seq"), lax.axis_index("mp"), lax.axis_index("dp")
    lo, z = lax.div(seq, NZ), lax.rem(seq, NZ)
    y, c = lax.div(mp, 2), lax.rem(mp, 2)

    def zmod(a):
        return lax.rem(a + 2 * NZ, NZ)

    def ymod(a):
        return lax.rem(a + 2 * NY, NY)

    def dev(s, m, d):
        return {"seq": s, "mp": m, "dp": d}

    zr = dev(lo * NZ + zmod(z + 1), mp, dp)
    zl = dev(lo * NZ + zmod(z - 1), mp, dp)
    other_seq = (1 - lo) * NZ + z
    xr_dev = dev(other_seq, mp, lax.rem(dp + lo, 2))
    xl_dev = dev(other_seq, mp, lax.rem(dp + 1 - lo, 2))
    pair = dev(other_seq, mp, dp)
    core = dev(seq, 2 * y + 1 - c, dp)
    ys = [dev(seq, 2 * ymod(y + d) + c, dp) for d in (1, 2, 3)]
    after = dev(lax.rem(seq + 1, 2 * NZ), mp, dp)
    before = dev(lax.rem(seq + 2 * NZ - 1, 2 * NZ), mp, dp)

    pending = []

    def send(src, dst, ssem, rsem, to):
        d = pltpu.make_async_remote_copy(
            src_ref=src, dst_ref=dst, send_sem=ssem, recv_sem=rsem, device_id=to, device_id_type=MESH
        )
        d.start()
        pending.append(d)

    def arrived(dst, ssem, rsem, frm):
        pltpu.make_async_remote_copy(
            src_ref=dst, dst_ref=dst, send_sem=ssem, recv_sem=rsem, device_id=frm, device_id_type=MESH
        ).wait_recv()

    def local(src, dst, i):
        d = pltpu.make_async_copy(src, dst, loc.at[i])
        d.start()
        return d

    own_cols, far_cols = pl.ds(pl.multiple_of(lo * HD, HD), HD), pl.ds(pl.multiple_of((1 - lo) * HD, HD), HD)
    own_rows = pl.ds(pl.multiple_of(lo * TOK, TOK), TOK)
    far_rows = pl.ds(pl.multiple_of((1 - lo) * TOK, TOK), TOK)

    def col_slot(ref):
        return lambda j: ref.at[:, pl.ds(pl.multiple_of(j * 128, 128), 128)]

    def row_slot(ref):
        return lambda j: ref.at[pl.ds(pl.multiple_of(j * 128, 128), 128), :]

    slots = [col_slot(wo), row_slot(cv), col_slot(co), row_slot(fi), col_slot(fd)]
    my_rows = pl.ds(pl.multiple_of(seq * 128, 128), 128)
    lk = local(k_hbm.at[:, own_cols], kb.at[z, own_rows, :], 0)
    lv = local(v_hbm.at[:, own_cols], vb.at[z, own_rows, :], 1)
    lq = local(q_hbm.at[:, own_cols], qb.at[own_rows, :], 2)
    own = [
        [local(wo_hbm, slots[0](seq), 3)],
        [local(cval_hbm, cv.at[my_rows, 0:256], 4), local(cgate_hbm, cv.at[my_rows, 256:512], 5)],
        [local(co_hbm, slots[2](seq), 6)],
        [local(fi_hbm, slots[3](seq), 7)],
        [local(fd_hbm, slots[4](seq), 8)],
    ]
    lres = local(res_hbm.at[pl.ds(pl.multiple_of(mp * ROWS, ROWS), ROWS), :], res, 9)

    bar = pltpu.get_barrier_semaphore()
    peers = [zr, zl, xr_dev, xl_dev, core, *ys, after, before]
    for p in peers:
        pl.semaphore_signal(bar, inc=1, device_id=p, device_id_type=MESH)
    pl.semaphore_wait(bar, len(peers))

    hbm_of, buf_of, hops_of = (k_hbm, v_hbm), (kb, vb), (HOPS_A, HOPS_B)
    for i, (src, dst) in enumerate(
        ((k_hbm, kb.at[z, own_rows, :]), (v_hbm, vb.at[z, own_rows, :]), (q_hbm, qb.at[own_rows, :]))
    ):
        send(src.at[:, far_cols], dst, qx_s.at[i], qx_r.at[i], pair)
    for a in (0, 1):
        for w, to in ((RIGHT, zr), (LEFT, zl)):
            send(hbm_of[a].at[:, own_cols], buf_of[a].at[z, own_rows, :], kv1_s.at[a, w, 0], kv1_r.at[a, w, 0], to)
    for a in (0, 1):
        half = buf_of[a].at[z, far_rows, :]
        arrived(half, qx_s.at[a], qx_r.at[a], pair)
        for w, to in ((RIGHT, zr), (LEFT, zl)):
            send(half, half, kv1_s.at[a, w, 1], kv1_r.at[a, w, 1], to)

    def kv_relay(s):
        for a in (0, 1):
            for w, frm, to, sign in ((RIGHT, zl, zr, -1), (LEFT, zr, zl, 1)):
                if s > hops_of[a][w]:
                    continue
                slot = zmod(z + sign * s)
                if s == 1:
                    for half, rows in ((0, own_rows), (1, far_rows)):
                        arrived(buf_of[a].at[slot, rows, :], kv1_s.at[a, w, half], kv1_r.at[a, w, half], frm)
                else:
                    arrived(buf_of[a].at[slot], kv_s.at[a, w, s - 2], kv_r.at[a, w, s - 2], frm)
                if s + 1 <= hops_of[a][w]:
                    ref = buf_of[a].at[slot]
                    send(ref, ref, kv_s.at[a, w, s - 1], kv_r.at[a, w, s - 1], to)

    hops_w = [HOPS_A, HOPS_B, HOPS_B, HOPS_A, HOPS_B]

    def x_way(p, k):
        return RIGHT if (p + k) % 2 == 0 else LEFT

    def x_send(p, k, shard):
        w = x_way(p, k)
        ref = slots[p](lo * NZ + shard)
        send(ref, ref, wx_s.at[p, k], wx_r.at[p, k], xr_dev if w == RIGHT else xl_dev)

    def begin(p):
        for d in own[p]:
            d.wait()
        ref = slots[p](seq)
        for w, to in ((RIGHT, zr), (LEFT, zl)):
            send(ref, ref, wz_s.at[p, w, 0], wz_r.at[p, w, 0], to)
        x_send(p, 0, z)

    def relay(p, s):
        for w, frm, to, sign in ((RIGHT, zl, zr, -1), (LEFT, zr, zl, 1)):
            if s > hops_w[p][w]:
                continue
            shard = zmod(z + sign * s)
            ref = slots[p](lo * NZ + shard)
            arrived(ref, wz_s.at[p, w, s - 1], wz_r.at[p, w, s - 1], frm)
            if s + 1 <= hops_w[p][w]:
                send(ref, ref, wz_s.at[p, w, s], wz_r.at[p, w, s], to)
            x_send(p, 7 if s == 4 else 2 * s - 1 + w, shard)

    def weights_done(p):
        for k in range(8):
            shard = z if k == 0 else z + 4 if k == 7 else z - (k + 1) // 2 if k % 2 else z + k // 2
            frm = xl_dev if x_way(p, k) == RIGHT else xr_dev
            arrived(slots[p]((1 - lo) * NZ + zmod(shard)), wx_s.at[p, k], wx_r.at[p, k], frm)

    todo = [
        (1, 1), (1, 2), (3, 0), (2, 1), (1, 3), (2, 2), (1, 4), (2, 3), (3, 1), (2, 4), (4, 0), (3, 2),
        (4, 1), (3, 3), (4, 2), (3, 4), (4, 3), (4, 4),
    ]

    def pump(n):
        for _ in range(min(n, len(todo))):
            p, s = todo.pop(0)
            if s == 0:
                begin(p)
            else:
                relay(p, s)

    def need(p):
        while any(q == p for q, _ in todo):
            pump(1)
        weights_done(p)

    scale2 = math.log2(math.e) / math.sqrt(HD)

    def attend(slot, first=False):
        def body(i, carry):
            rows = pl.ds(pl.multiple_of(i * BQ, BQ), BQ)
            s = lax.dot_general(
                qb[rows, :], kb[slot], (((1,), (1,)), ((), ())), preferred_element_type=F32
            )
            top = jnp.max(s, axis=1, keepdims=True)
            if not first:
                old = m_s[rows, :]
                top = jnp.maximum(top, old[:, :1])
            p = jnp.exp2((s - top) * scale2)
            part = p[:, 0:128]
            for t in range(1, 6):
                part = part + p[:, t * 128 : (t + 1) * 128]
            out = jnp.dot(p.astype(BF), vb[slot], preferred_element_type=F32)
            if not first:
                shrink = jnp.exp2((old - top) * scale2)
                part = part + l_s[rows, :] * shrink
                out = out + acc[rows, :] * shrink
            m_s[rows, :] = jnp.broadcast_to(top, (BQ, 128))
            l_s[rows, :] = part
            acc[rows, :] = out
            return carry

        lax.fori_loop(0, 2 * TOK // BQ, body, 0)

    begin(0)
    arrived(qb.at[far_rows, :], qx_s.at[2], qx_r.at[2], pair)
    lq.wait()
    lk.wait()
    lv.wait()
    attend(z, first=True)
    for s in (1, 2, 3):
        kv_relay(s)
        relay(0, s)
        if s == 2:
            begin(1)
        if s == 3:
            begin(2)
        attend(zmod(z - s))
        attend(zmod(z + s))
    kv_relay(4)
    relay(0, 4)
    attend(zmod(z + 4))

    def finish(rows, blocks):
        o = acc[rows, :] / jnp.sum(l_s[rows, :], axis=1, keepdims=True)
        ob[blocks] = o.astype(BF).reshape(8, ROWS, HD)

    far_blocks, own_blocks = pl.ds((1 - lo) * 8, 8), pl.ds(lo * 8, 8)
    finish(far_rows, far_blocks)
    send(ob.at[far_blocks], ho.at[:, :, own_cols], o_s, o_r, pair)
    finish(own_rows, own_blocks)
    lo_copy = local(ob.at[own_blocks], ho.at[:, :, own_cols], 10)
    for i in range(3):
        for u in range(8):
            mrow[i : i + 1, u * 128 : (u + 1) * 128] = jnp.full((1, 128), mask_ref[i, u].astype(F32))
    lres.wait()
    stream[...] = res[...].astype(F32)
    lo_copy.wait()
    pump(1)
    arrived(ho.at[:, :, far_cols], o_s, o_r, pair)

    def branch(n, left, weight, factor, pumps):
        for mine in (False, True):
            side = c if mine else 1 - c
            lhs = jnp.concatenate([left[2 * b + side] for b in range(NY)], axis=0)
            for j in range(4):
                cols = slice(j * 512, (j + 1) * 512)
                prod = jnp.dot(lhs, weight[:, cols], preferred_element_type=F32).reshape(NY, ROWS, 512)
                if mine:
                    ps[:, :, cols] = prod
                else:
                    xs[n, :, :, cols] = prod.astype(BF)
            if not mine:
                send(xs.at[n], xr.at[n], pc_s.at[n], pc_r.at[n], core)
        pump(pumps[0])
        arrived(xr.at[n], pc_s.at[n], pc_r.at[n], core)
        for d in (2, 1, 3):
            b = ymod(y + d)
            rs[n, d - 1] = (ps[b] + xr[n, b].astype(F32)).astype(BF)
            send(rs.at[n, d - 1], rr.at[n, d - 1], rx_s.at[n, d - 1], rx_r.at[n, d - 1], ys[d - 1])
        total = ps[y] + xr[n, y].astype(F32)
        pump(pumps[1])
        for d in (1, 3, 2):
            arrived(rr.at[n, d - 1], rx_s.at[n, d - 1], rx_r.at[n, d - 1], ys[3 - d])
            total = total + rr[n, d - 1].astype(F32)
        new = stream[...] + factor * total
        stream[...] = new
        return layer_norm(new)

    def share(n, rows, pumps):
        nb[n, mp] = rows.astype(BF)
        mine = nb.at[n, mp]
        for d in (2, 1, 3):
            send(mine, mine, ag_s.at[n, d - 1], ag_r.at[n, d - 1], ys[d - 1])
        send(mine, mine, agc_s.at[n, 0], agc_r.at[n, 0], core)
        pump(pumps)
        for d in (1, 3, 2):
            got = nb.at[n, 2 * ymod(y - d) + c]
            arrived(got, ag_s.at[n, d - 1], ag_r.at[n, d - 1], ys[3 - d])
            send(got, got, agc_s.at[n, d], agc_r.at[n, d], core)
        for d in (0, 1, 3, 2):
            arrived(nb.at[n, 2 * ymod(y - d) + 1 - c], agc_s.at[n, d], agc_r.at[n, d], core)

    need(0)
    norm_one = branch(0, ho, wo, 1.0, (2, 3))
    share(0, norm_one, 3)

    need(1)
    lhs = nb[0].reshape(TOK, D)
    value = jnp.dot(lhs, cv[:, 0:256], preferred_element_type=F32)
    gate = jnp.dot(lhs, cv[:, 256:512], preferred_element_type=F32)
    gated = (value * jax.nn.sigmoid(gate)).astype(BF)
    gs[0] = gated[TOK - 16 :, :]
    gs[1] = gated[:16, :]
    send(gs.at[0], gr.at[0], h_s.at[0], h_r.at[0], after)
    send(gs.at[1], gr.at[1], h_s.at[1], h_r.at[1], before)
    gp[16 : 16 + TOK, :] = gated.astype(F32)
    arrived(gr.at[0], h_s.at[0], h_r.at[0], before)
    arrived(gr.at[1], h_s.at[1], h_r.at[1], after)
    gp[0:16, :] = jnp.where(seq > 0, gr[0].astype(F32), 0.0)
    gp[16 + TOK :, :] = jnp.where(seq < 2 * NZ - 1, gr[1].astype(F32), 0.0)
    for r in range(8):
        sh[r] = gp[r + 1 : r + 1 + TOK + 24, :]

    def depth(i, carry):
        total = jnp.zeros((96, 256), F32)
        for t in range(TAPS):
            total = total + dk_ref[t : t + 1, :] * sh[t % 8, pl.ds(pl.multiple_of(i * 96 + t // 8 * 8, 8), 96), :]
        act[pl.ds(2 * i, 2)] = (total * jax.nn.sigmoid(total)).astype(BF).reshape(2, ROWS, 256)
        return carry

    lax.fori_loop(0, 4, depth, 0)
    need(2)
    norm_two = branch(1, act, co, 1.0, (1, 2))
    share(1, norm_two, 2)

    need(3)

    def ffn(j, carry):
        cols = pl.ds(pl.multiple_of(j * 256, 256), 256)
        pre = jnp.dot(nb[1].reshape(TOK, D), fi[:, cols], preferred_element_type=F32)
        h = (pre * jax.nn.sigmoid(pre)).reshape(3, 128, 256) * mrow[:, cols][:, None, :]
        hid[:, :, cols] = h.astype(BF).reshape(8, ROWS, 256)
        return carry

    lax.fori_loop(0, 4, ffn, 0)
    need(4)
    out_ref[...] = branch(2, hid, fd, 0.5, (0, 0))
    for d in pending:
        d.wait_send()


def on_device(*args):
    dma = pltpu.SemaphoreType.DMA
    any_spec = pl.BlockSpec(memory_space=pl.ANY)
    vmem, smem = pl.BlockSpec(memory_space=pltpu.VMEM), pl.BlockSpec(memory_space=pltpu.SMEM)
    v = pltpu.VMEM
    return pl.pallas_call(
        block_kernel,
        out_shape=jax.ShapeDtypeStruct((ROWS, D), F32),
        in_specs=[any_spec] * 7 + [vmem] + [any_spec] * 3 + [smem],
        out_specs=vmem,
        scratch_shapes=[
            v((2 * TOK, HD), BF), v((NZ, 2 * TOK, HD), BF), v((NZ, 2 * TOK, HD), BF),
            v((2 * TOK, 128), F32), v((2 * TOK, 128), F32), v((2 * TOK, HD), F32),
            v((16, ROWS, HD), BF), v((8, ROWS, 256), BF),
            v((256, D), BF), v((D, 512), BF), v((256, D), BF), v((D, 1024), BF), v((1024, D), BF),
            v((ROWS, D), BF), v((ROWS, D), F32), v((NY, ROWS, D), F32),
            v((3, NY, ROWS, D), BF), v((3, NY, ROWS, D), BF), v((3, 3, ROWS, D), BF), v((3, 3, ROWS, D), BF),
            v((2, 8, ROWS, D), BF),
            v((TOK + 32, 256), F32), v((8, TOK + 24, 256), F32), v((2, 16, 256), BF), v((2, 16, 256), BF),
            v((8, ROWS, 256), BF), v((8, ROWS, 1024), BF), v((3, 1024), F32),
            dma((11,)), dma((3,)), dma((3,)), dma((2, 2, 2)), dma((2, 2, 2)), dma((2, 2, 3)), dma((2, 2, 3)),
            dma((5, 2, 4)), dma((5, 2, 4)), dma((5, 8)), dma((5, 8)), dma(()), dma(()),
            dma((3,)), dma((3,)), dma((3, 3)), dma((3, 3)), dma((2, 3)), dma((2, 3)), dma((2, 4)), dma((2, 4)),
            dma((2,)), dma((2,)),
        ],
        compiler_params=pltpu.CompilerParams(
            collective_id=0, has_side_effects=True, vmem_limit_bytes=60 * 1024 * 1024
        ),
        name="block",
    )(*args)


def solution(mesh):
    in_specs = (
        P(("dp", "seq"), None),
        P(("dp", "seq"), "mp"),
        P(("dp", "seq"), "mp"),
        P(("dp", "seq"), "mp"),
        P("mp", "seq"),
        P("seq", "mp"),
        P("seq", "mp"),
        P(None, "mp"),
        P("mp", "seq"),
        P("seq", "mp"),
        P("mp", "seq"),
        P(("dp", "seq"), "mp"),
    )
    out_specs = P(("dp", "seq", "mp"), None)
    return jax.shard_map(on_device, mesh=mesh, in_specs=in_specs, out_specs=out_specs, check_vma=False)
```

```python
import math

import jax
import jax.numpy as jnp
from jax import lax
from jax.experimental import pallas as pl
from jax.experimental.pallas import tpu as pltpu
from jax.sharding import PartitionSpec as P

MESH = pl.DeviceIdType.MESH
BF, F32 = jnp.bfloat16, jnp.float32
HD = 128
NZ = 8
NY = 4
TOK = 384
ROWS = 48
D = 2048
EPS = 1e-05
TAPS = 31
BQ = 256
RIGHT, LEFT = 0, 1
HOPS_A, HOPS_B = (4, 3), (3, 4)
CHUNKS = ROWS // 16
RELAYS = [
    (3, 0), (1, 1), (2, 1), (3, 1), (4, 0), (1, 2), (2, 2), (3, 2), (4, 1), (1, 3), (2, 3), (3, 3), (4, 2), (1, 4),
    (2, 4), (5, 0), (3, 4), (4, 3), (6, 0), (5, 1), (4, 4), (6, 1), (5, 2), (6, 2), (5, 3), (6, 3), (5, 4), (6, 4),
]
PUMPS = [3] + [1, 1, 1, 1, 1, 1, 1, 1] + [1, 1] + [1, 1, 1, 1, 1, 1, 1, 1] + [0, 0, 0, 0]


def layer_norm(x):
    mean = jnp.mean(x, axis=-1, keepdims=True)
    cen = x - mean
    var = jnp.mean(cen * cen, axis=-1, keepdims=True)
    return cen * lax.rsqrt(var + EPS)


def block_kernel(
    res_hbm, q_hbm, k_hbm, v_hbm, wo_hbm, cval_hbm, cgate_hbm, dk_ref, co_hbm, fi_hbm, fd_hbm, mask_ref,
    out_ref,
    qb, kb, vb, m_s, l_s, acc, ob, ho, wo, cv, co, fi, fd, res, stream, ps, xs, xr, rs, rr, nb,
    gp, sh, gs, gr, act, hid, mrow,
    loc, qx_s, qx_r, kv1_s, kv1_r, kv_s, kv_r, wz_s, wz_r, wx_s, wx_r, o_s, o_r,
    pc_s, pc_r, rx_s, rx_r, ag_s, ag_r, agc_s, agc_r, h_s, h_r,
):
    seq, mp, dp = lax.axis_index("seq"), lax.axis_index("mp"), lax.axis_index("dp")
    lo, z = lax.div(seq, NZ), lax.rem(seq, NZ)
    y, c = lax.div(mp, 2), lax.rem(mp, 2)

    def zmod(a):
        return lax.rem(a + 2 * NZ, NZ)

    def ymod(a):
        return lax.rem(a + 2 * NY, NY)

    def dev(s, m, d):
        return {"seq": s, "mp": m, "dp": d}

    zr = dev(lo * NZ + zmod(z + 1), mp, dp)
    zl = dev(lo * NZ + zmod(z - 1), mp, dp)
    other_seq = (1 - lo) * NZ + z
    xr_dev = dev(other_seq, mp, lax.rem(dp + lo, 2))
    xl_dev = dev(other_seq, mp, lax.rem(dp + 1 - lo, 2))
    pair = dev(other_seq, mp, dp)
    core = dev(seq, 2 * y + 1 - c, dp)
    ys = [dev(seq, 2 * ymod(y + d) + c, dp) for d in (1, 2, 3)]
    after = dev(lax.rem(seq + 1, 2 * NZ), mp, dp)
    before = dev(lax.rem(seq + 2 * NZ - 1, 2 * NZ), mp, dp)

    pending = []

    def send(src, dst, ssem, rsem, to):
        d = pltpu.make_async_remote_copy(
            src_ref=src, dst_ref=dst, send_sem=ssem, recv_sem=rsem, device_id=to, device_id_type=MESH
        )
        d.start()
        pending.append(d)

    def arrived(dst, ssem, rsem, frm):
        pltpu.make_async_remote_copy(
            src_ref=dst, dst_ref=dst, send_sem=ssem, recv_sem=rsem, device_id=frm, device_id_type=MESH
        ).wait_recv()

    def local(src, dst, i):
        d = pltpu.make_async_copy(src, dst, loc.at[i])
        d.start()
        return d

    own_cols, far_cols = pl.ds(pl.multiple_of(lo * HD, HD), HD), pl.ds(pl.multiple_of((1 - lo) * HD, HD), HD)
    own_rows = pl.ds(pl.multiple_of(lo * TOK, TOK), TOK)
    far_rows = pl.ds(pl.multiple_of((1 - lo) * TOK, TOK), TOK)

    def col_slot(ref):
        return lambda j: ref.at[:, pl.ds(pl.multiple_of(j * 128, 128), 128)]

    def row_slot(ref):
        return lambda j: ref.at[pl.ds(pl.multiple_of(j * 128, 128), 128), :]

    slots = [
        col_slot(wo), row_slot(cv), col_slot(co), row_slot(fi.at[:, 0:512]), row_slot(fi.at[:, 512:1024]),
        col_slot(fd.at[0:512, :]), col_slot(fd.at[512:1024, :]),
    ]
    my_rows = pl.ds(pl.multiple_of(seq * 128, 128), 128)
    lk = local(k_hbm.at[:, own_cols], kb.at[z, own_rows, :], 0)
    lv = local(v_hbm.at[:, own_cols], vb.at[z, own_rows, :], 1)
    lq = local(q_hbm.at[:, own_cols], qb.at[own_rows, :], 2)
    own = [
        [local(wo_hbm, slots[0](seq), 3)],
        [local(cval_hbm, cv.at[my_rows, 0:256], 4), local(cgate_hbm, cv.at[my_rows, 256:512], 5)],
        [local(co_hbm, slots[2](seq), 6)],
        [local(fi_hbm.at[:, 0:512], slots[3](seq), 7)],
        [local(fi_hbm.at[:, 512:1024], slots[4](seq), 8)],
        [local(fd_hbm.at[0:512, :], slots[5](seq), 9)],
        [local(fd_hbm.at[512:1024, :], slots[6](seq), 10)],
    ]
    lres = local(res_hbm.at[pl.ds(pl.multiple_of(mp * ROWS, ROWS), ROWS), :], res, 11)

    bar = pltpu.get_barrier_semaphore()
    peers = [zr, zl, xr_dev, xl_dev, core, *ys, after, before]
    for p in peers:
        pl.semaphore_signal(bar, inc=1, device_id=p, device_id_type=MESH)
    pl.semaphore_wait(bar, len(peers))

    hbm_of, buf_of, hops_of = (k_hbm, v_hbm), (kb, vb), (HOPS_A, HOPS_B)
    for i, (src, dst) in enumerate(
        ((k_hbm, kb.at[z, own_rows, :]), (v_hbm, vb.at[z, own_rows, :]), (q_hbm, qb.at[own_rows, :]))
    ):
        send(src.at[:, far_cols], dst, qx_s.at[i], qx_r.at[i], pair)
    for a in (0, 1):
        for w, to in ((RIGHT, zr), (LEFT, zl)):
            send(hbm_of[a].at[:, own_cols], buf_of[a].at[z, own_rows, :], kv1_s.at[a, w, 0], kv1_r.at[a, w, 0], to)

    def pass_half(a):
        half = buf_of[a].at[z, far_rows, :]
        arrived(half, qx_s.at[a], qx_r.at[a], pair)
        for w, to in ((RIGHT, zr), (LEFT, zl)):
            send(half, half, kv1_s.at[a, w, 1], kv1_r.at[a, w, 1], to)

    def kv_relay(a, s):
        for w, frm, to, sign in ((RIGHT, zl, zr, -1), (LEFT, zr, zl, 1)):
            if s > hops_of[a][w]:
                continue
            slot = zmod(z + sign * s)
            if s == 1:
                for half, rows in ((0, own_rows), (1, far_rows)):
                    arrived(buf_of[a].at[slot, rows, :], kv1_s.at[a, w, half], kv1_r.at[a, w, half], frm)
            else:
                arrived(buf_of[a].at[slot], kv_s.at[a, w, s - 2], kv_r.at[a, w, s - 2], frm)
            if s + 1 <= hops_of[a][w]:
                ref = buf_of[a].at[slot]
                send(ref, ref, kv_s.at[a, w, s - 1], kv_r.at[a, w, s - 1], to)

    hops_w = [HOPS_A, HOPS_B, HOPS_A, HOPS_A, HOPS_B, HOPS_A, HOPS_B]

    def x_way(p, k):
        return RIGHT if (p + k) % 2 == 0 else LEFT

    def x_send(p, k, shard):
        w = x_way(p, k)
        ref = slots[p](lo * NZ + shard)
        send(ref, ref, wx_s.at[p, k], wx_r.at[p, k], xr_dev if w == RIGHT else xl_dev)

    def begin(p):
        ref = slots[p](seq)
        for w, to in ((RIGHT, zr), (LEFT, zl)):
            send(ref, ref, wz_s.at[p, w, 0], wz_r.at[p, w, 0], to)

    def relay(p, s):
        for w, frm, to, sign in ((RIGHT, zl, zr, -1), (LEFT, zr, zl, 1)):
            if s > hops_w[p][w]:
                continue
            shard = zmod(z + sign * s)
            ref = slots[p](lo * NZ + shard)
            arrived(ref, wz_s.at[p, w, s - 1], wz_r.at[p, w, s - 1], frm)
            if s + 1 <= hops_w[p][w]:
                send(ref, ref, wz_s.at[p, w, s], wz_r.at[p, w, s], to)
            x_send(p, 7 if s == 4 else 2 * s - 1 + w, shard)

    def weights_done(p):
        for k in range(8):
            shard = z if k == 0 else z + 4 if k == 7 else z - (k + 1) // 2 if k % 2 else z + k // 2
            frm = xl_dev if x_way(p, k) == RIGHT else xr_dev
            arrived(slots[p]((1 - lo) * NZ + zmod(shard)), wx_s.at[p, k], wx_r.at[p, k], frm)

    todo = list(RELAYS)
    counts = list(PUMPS)

    def pump(n=None):
        for _ in range(min(counts.pop(0) if n is None else n, len(todo))):
            p, s = todo.pop(0)
            if s == 0:
                begin(p)
            else:
                relay(p, s)

    def need(p):
        while any(q == p for q, _ in todo):
            pump(1)
        weights_done(p)

    scale2 = math.log2(math.e) / math.sqrt(HD)

    def attend(slot, first=False):
        def body(i, carry):
            rows = pl.ds(pl.multiple_of(i * BQ, BQ), BQ)
            s = lax.dot_general(
                qb[rows, :], kb[slot], (((1,), (1,)), ((), ())), preferred_element_type=F32
            )
            top = jnp.max(s, axis=1, keepdims=True)
            if not first:
                old = m_s[rows, :]
                top = jnp.maximum(top, old[:, :1])
            p = jnp.exp2((s - top) * scale2)
            part = p[:, 0:128]
            for t in range(1, 6):
                part = part + p[:, t * 128 : (t + 1) * 128]
            out = jnp.dot(p.astype(BF), vb[slot], preferred_element_type=F32)
            if not first:
                shrink = jnp.exp2((old - top) * scale2)
                part = part + l_s[rows, :] * shrink
                out = out + acc[rows, :] * shrink
            m_s[rows, :] = jnp.broadcast_to(top, (BQ, 128))
            l_s[rows, :] = part
            acc[rows, :] = out
            return carry

        lax.fori_loop(0, 2 * TOK // BQ, body, 0)

    for d in own[0]:
        d.wait()
    begin(0)
    pass_half(0)
    pass_half(1)
    for p in range(len(slots)):
        if p:
            for d in own[p]:
                d.wait()
        x_send(p, 0, z)
    lq.wait()
    lk.wait()
    lv.wait()
    arrived(qb.at[far_rows, :], qx_s.at[2], qx_r.at[2], pair)
    attend(z, first=True)
    for s in (1, 2, 3, 4):
        kv_relay(0, s)
        if s > 1:
            attend(zmod(z + s - 1))
        kv_relay(1, s)
        relay(0, s)
        if s in (2, 3):
            begin(s - 1)
        attend(zmod(z - s))
    def finish(rows, blocks):
        o = acc[rows, :] / jnp.sum(l_s[rows, :], axis=1, keepdims=True)
        ob[blocks] = o.astype(BF).reshape(8, ROWS, HD)

    far_blocks, own_blocks = pl.ds((1 - lo) * 8, 8), pl.ds(lo * 8, 8)
    finish(far_rows, far_blocks)
    send(ob.at[far_blocks], ho.at[:, :, own_cols], o_s, o_r, pair)
    finish(own_rows, own_blocks)
    lo_copy = local(ob.at[own_blocks], ho.at[:, :, own_cols], 12)
    for i in range(3):
        for u in range(8):
            mrow[i : i + 1, u * 128 : (u + 1) * 128] = jnp.full((1, 128), mask_ref[i, u].astype(F32))
    lres.wait()
    stream[...] = res[...].astype(F32)
    lo_copy.wait()
    pump()
    arrived(ho.at[:, :, far_cols], o_s, o_r, pair)

    def branch(n, left, weight, factor):
        for mine in (False, True):
            side = c if mine else 1 - c
            lhs = jnp.concatenate([left[2 * b + side] for b in range(NY)], axis=0)
            for j in range(4):
                cols = slice(j * 512, (j + 1) * 512)
                prod = jnp.dot(lhs, weight[:, cols], preferred_element_type=F32).reshape(NY, ROWS, 512)
                for r in range(CHUNKS):
                    chunk = prod[:, r * 16 : (r + 1) * 16]
                    if mine:
                        ps[r, :, :, cols] = chunk
                    else:
                        xs[n, r, :, :, cols] = chunk.astype(BF)
            if not mine:
                for r in range(CHUNKS):
                    send(xs.at[n, r], xr.at[n, r], pc_s.at[n, r], pc_r.at[n, r], core)
                pump()
        for r in range(CHUNKS):
            arrived(xr.at[n, r], pc_s.at[n, r], pc_r.at[n, r], core)
            for d in (2, 1, 3):
                b = ymod(y + d)
                rs[n, r, d - 1] = (ps[r, b] + xr[n, r, b].astype(F32)).astype(BF)
                send(rs.at[n, r, d - 1], rr.at[n, r, d - 1], rx_s.at[n, r, d - 1], rx_r.at[n, r, d - 1], ys[d - 1])
        for r in range(CHUNKS):
            pump()
            rows = slice(r * 16, (r + 1) * 16)
            total = ps[r, y] + xr[n, r, y].astype(F32)
            for d in (1, 3, 2):
                arrived(rr.at[n, r, d - 1], rx_s.at[n, r, d - 1], rx_r.at[n, r, d - 1], ys[3 - d])
                total = total + rr[n, r, d - 1].astype(F32)
            new = stream[rows, :] + factor * total
            if n == 2:
                out_ref[rows, :] = layer_norm(new)
                continue
            stream[rows, :] = new
            mine = nb.at[n, mp, rows]
            nb[n, mp, rows] = layer_norm(new).astype(BF)
            for d in (2, 1, 3):
                send(mine, mine, ag_s.at[n, r, d - 1], ag_r.at[n, r, d - 1], ys[d - 1])
            send(mine, mine, agc_s.at[n, r, 0], agc_r.at[n, r, 0], core)
        if n == 2:
            return
        for r in range(CHUNKS):
            pump()
            rows = slice(r * 16, (r + 1) * 16)
            for d in (1, 3, 2):
                got = nb.at[n, 2 * ymod(y - d) + c, rows]
                arrived(got, ag_s.at[n, r, d - 1], ag_r.at[n, r, d - 1], ys[3 - d])
                send(got, got, agc_s.at[n, r, d], agc_r.at[n, r, d], core)
        pump()
        for r in range(CHUNKS):
            rows = slice(r * 16, (r + 1) * 16)
            for d in (0, 1, 3, 2):
                arrived(nb.at[n, 2 * ymod(y - d) + 1 - c, rows], agc_s.at[n, r, d], agc_r.at[n, r, d], core)

    need(0)
    branch(0, ho, wo, 1.0)

    need(1)

    def glu(rows):
        value = jnp.dot(rows, cv[:, 0:256], preferred_element_type=F32)
        gate = jnp.dot(rows, cv[:, 256:512], preferred_element_type=F32)
        return (value * jax.nn.sigmoid(gate)).astype(BF)

    edge = glu(jnp.concatenate([nb[0, 7, ROWS - 16 :, :], nb[0, 0, :16, :]], axis=0))
    gs[0] = edge[:16]
    gs[1] = edge[16:]
    send(gs.at[0], gr.at[0], h_s.at[0], h_r.at[0], after)
    send(gs.at[1], gr.at[1], h_s.at[1], h_r.at[1], before)
    gp[16 : 16 + TOK, :] = glu(nb[0].reshape(TOK, D)).astype(F32)
    pump()
    arrived(gr.at[0], h_s.at[0], h_r.at[0], before)
    arrived(gr.at[1], h_s.at[1], h_r.at[1], after)
    gp[0:16, :] = jnp.where(seq > 0, gr[0].astype(F32), 0.0)
    gp[16 + TOK :, :] = jnp.where(seq < 2 * NZ - 1, gr[1].astype(F32), 0.0)
    for r in range(8):
        sh[r] = gp[r + 1 : r + 1 + TOK + 24, :]

    def depth(i, carry):
        total = jnp.zeros((96, 256), F32)
        for t in range(TAPS):
            total = total + dk_ref[t : t + 1, :] * sh[t % 8, pl.ds(pl.multiple_of(i * 96 + t // 8 * 8, 8), 96), :]
        act[pl.ds(2 * i, 2)] = (total * jax.nn.sigmoid(total)).astype(BF).reshape(2, ROWS, 256)
        return carry

    lax.fori_loop(0, 4, depth, 0)
    pump()
    need(2)
    branch(1, act, co, 1.0)

    need(3)
    need(4)

    def ffn(j, carry):
        cols = pl.ds(pl.multiple_of(j * 256, 256), 256)
        pre = jnp.dot(nb[1].reshape(TOK, D), fi[:, cols], preferred_element_type=F32)
        h = (pre * jax.nn.sigmoid(pre)).reshape(3, 128, 256) * mrow[:, cols][:, None, :]
        hid[:, :, cols] = h.astype(BF).reshape(8, ROWS, 256)
        return carry

    lax.fori_loop(0, 4, ffn, 0)
    need(5)
    need(6)
    branch(2, hid, fd, 0.5)
    for d in pending:
        d.wait_send()


def on_device(*args):
    dma = pltpu.SemaphoreType.DMA
    any_spec = pl.BlockSpec(memory_space=pl.ANY)
    vmem, smem = pl.BlockSpec(memory_space=pltpu.VMEM), pl.BlockSpec(memory_space=pltpu.SMEM)
    v = pltpu.VMEM
    return pl.pallas_call(
        block_kernel,
        out_shape=jax.ShapeDtypeStruct((ROWS, D), F32),
        in_specs=[any_spec] * 7 + [vmem] + [any_spec] * 3 + [smem],
        out_specs=vmem,
        scratch_shapes=[
            v((2 * TOK, HD), BF), v((NZ, 2 * TOK, HD), BF), v((NZ, 2 * TOK, HD), BF),
            v((2 * TOK, 128), F32), v((2 * TOK, 128), F32), v((2 * TOK, HD), F32),
            v((16, ROWS, HD), BF), v((8, ROWS, 256), BF),
            v((256, D), BF), v((D, 512), BF), v((256, D), BF), v((D, 1024), BF), v((1024, D), BF),
            v((ROWS, D), BF), v((ROWS, D), F32), v((CHUNKS, NY, 16, D), F32),
            v((3, CHUNKS, NY, 16, D), BF), v((3, CHUNKS, NY, 16, D), BF), v((3, CHUNKS, 3, 16, D), BF), v((3, CHUNKS, 3, 16, D), BF),
            v((2, 8, ROWS, D), BF),
            v((TOK + 32, 256), F32), v((8, TOK + 24, 256), F32), v((2, 16, 256), BF), v((2, 16, 256), BF),
            v((8, ROWS, 256), BF), v((8, ROWS, 1024), BF), v((3, 1024), F32),
            dma((13,)), dma((3,)), dma((3,)), dma((2, 2, 2)), dma((2, 2, 2)), dma((2, 2, 3)), dma((2, 2, 3)),
            dma((7, 2, 4)), dma((7, 2, 4)), dma((7, 8)), dma((7, 8)), dma(()), dma(()),
            dma((3, CHUNKS)), dma((3, CHUNKS)), dma((3, CHUNKS, 3)), dma((3, CHUNKS, 3)),
            dma((2, CHUNKS, 3)), dma((2, CHUNKS, 3)), dma((2, CHUNKS, 4)), dma((2, CHUNKS, 4)),
            dma((2,)), dma((2,)),
        ],
        compiler_params=pltpu.CompilerParams(
            collective_id=0, has_side_effects=True, vmem_limit_bytes=60 * 1024 * 1024
        ),
        name="block",
    )(*args)


def solution(mesh):
    in_specs = (
        P(("dp", "seq"), None),
        P(("dp", "seq"), "mp"),
        P(("dp", "seq"), "mp"),
        P(("dp", "seq"), "mp"),
        P("mp", "seq"),
        P("seq", "mp"),
        P("seq", "mp"),
        P(None, "mp"),
        P("mp", "seq"),
        P("seq", "mp"),
        P("mp", "seq"),
        P(("dp", "seq"), "mp"),
    )
    out_specs = P(("dp", "seq", "mp"), None)
    return jax.shard_map(on_device, mesh=mesh, in_specs=in_specs, out_specs=out_specs, check_vma=False)
```

```python
import math

import jax
import jax.numpy as jnp
from jax import lax
from jax.experimental import pallas as pl
from jax.experimental.pallas import tpu as pltpu
from jax.sharding import PartitionSpec as P

MESH = pl.DeviceIdType.MESH
BF, F32 = jnp.bfloat16, jnp.float32
HD = 128
NZ = 8
NY = 4
TOK = 384
ROWS = 48
D = 2048
EPS = 1e-05
TAPS = 31
RIGHT, LEFT = 0, 1
HOPS_A, HOPS_B = (4, 3), (3, 4)
CHUNKS, GROUPS = ROWS // 16, 4
RELAYS = [
    (1, 0), (3, 0), (1, 1), (2, 0), (4, 0), (2, 1), (1, 2), (3, 1), (1, 3), (4, 1), (2, 2), (5, 0),
    (1, 4), (2, 3), (4, 2), (6, 0), (2, 4), (3, 2), (5, 1), (3, 3), (4, 3), (6, 1), (5, 2), (3, 4),
    (6, 2), (4, 4), (6, 3), (5, 3), (6, 4), (5, 4),
]
PUMPS = [
    0, 0, 1, 1, 0, 3, 0, 3, 0, 4, 1, 0, 3, 2, 1, 0, 0, 4, 1, 2, 0, 2, 0, 2,
]


def layer_norm(x):
    mean = jnp.mean(x, axis=-1, keepdims=True)
    cen = x - mean
    var = jnp.mean(cen * cen, axis=-1, keepdims=True)
    return cen * lax.rsqrt(var + EPS)


def block_kernel(
    res_hbm, q_hbm, k_hbm, v_hbm, wo_hbm, cval_hbm, cgate_hbm, dk_ref, co_hbm, fi_hbm, fd_hbm, mask_ref,
    out_ref,
    qb, kb, vb, m_s, l_s, acc, ob, ho, wo, cv, co, fi, fd, res, stream, ps, xs, xr, rs, rr, ps3, xs3, xr3, rs3, rr3, nb,
    gp, sh, gs, gr, act, hid, mrow,
    loc, qx_s, qx_r, kv1_s, kv1_r, kv_s, kv_r, wz_s, wz_r, wx_s, wx_r, o_s, o_r,
    pc_s, pc_r, rx_s, rx_r, ag_s, ag_r, agc_s, agc_r, pc3_s, pc3_r, rx3_s, rx3_r, h_s, h_r,
):
    seq, mp, dp = lax.axis_index("seq"), lax.axis_index("mp"), lax.axis_index("dp")
    lo, z = lax.div(seq, NZ), lax.rem(seq, NZ)
    y, c = lax.div(mp, 2), lax.rem(mp, 2)

    def zmod(a):
        return lax.rem(a + 2 * NZ, NZ)

    def ymod(a):
        return lax.rem(a + 2 * NY, NY)

    def dev(s, m, d):
        return {"seq": s, "mp": m, "dp": d}

    zr = dev(lo * NZ + zmod(z + 1), mp, dp)
    zl = dev(lo * NZ + zmod(z - 1), mp, dp)
    other_seq = (1 - lo) * NZ + z
    xr_dev = dev(other_seq, mp, lax.rem(dp + lo, 2))
    xl_dev = dev(other_seq, mp, lax.rem(dp + 1 - lo, 2))
    pair = dev(other_seq, mp, dp)
    core = dev(seq, 2 * y + 1 - c, dp)
    ys = [dev(seq, 2 * ymod(y + d) + c, dp) for d in (1, 2, 3)]
    after = dev(lax.rem(seq + 1, 2 * NZ), mp, dp)
    before = dev(lax.rem(seq + 2 * NZ - 1, 2 * NZ), mp, dp)

    pending = []

    def send(src, dst, ssem, rsem, to):
        d = pltpu.make_async_remote_copy(
            src_ref=src, dst_ref=dst, send_sem=ssem, recv_sem=rsem, device_id=to, device_id_type=MESH
        )
        d.start()
        pending.append(d)

    def arrived(dst, ssem, rsem, frm):
        pltpu.make_async_remote_copy(
            src_ref=dst, dst_ref=dst, send_sem=ssem, recv_sem=rsem, device_id=frm, device_id_type=MESH
        ).wait_recv()

    def local(src, dst, i):
        d = pltpu.make_async_copy(src, dst, loc.at[i])
        d.start()
        return d

    own_cols, far_cols = pl.ds(pl.multiple_of(lo * HD, HD), HD), pl.ds(pl.multiple_of((1 - lo) * HD, HD), HD)
    own_rows = pl.ds(pl.multiple_of(lo * TOK, TOK), TOK)
    far_rows = pl.ds(pl.multiple_of((1 - lo) * TOK, TOK), TOK)

    def col_slot(ref):
        return lambda j: ref.at[:, pl.ds(pl.multiple_of(j * 128, 128), 128)]

    def row_slot(ref):
        return lambda j: ref.at[pl.ds(pl.multiple_of(j * 128, 128), 128), :]

    slots = [
        col_slot(wo), row_slot(cv), col_slot(co), row_slot(fi.at[:, 0:512]), row_slot(fi.at[:, 512:1024]),
        col_slot(fd.at[0:512, :]), col_slot(fd.at[512:1024, :]),
    ]
    my_rows = pl.ds(pl.multiple_of(seq * 128, 128), 128)
    lk = local(k_hbm.at[:, own_cols], kb.at[z, own_rows, :], 0)
    lv = local(v_hbm.at[:, own_cols], vb.at[z, own_rows, :], 1)
    lq = local(q_hbm.at[:, own_cols], qb.at[own_rows, :], 2)
    own = [
        [local(wo_hbm, slots[0](seq), 3)],
        [local(cval_hbm, cv.at[my_rows, 0:256], 4), local(cgate_hbm, cv.at[my_rows, 256:512], 5)],
        [local(co_hbm, slots[2](seq), 6)],
        [local(fi_hbm.at[:, 0:512], slots[3](seq), 7)],
        [local(fi_hbm.at[:, 512:1024], slots[4](seq), 8)],
        [local(fd_hbm.at[0:512, :], slots[5](seq), 9)],
        [local(fd_hbm.at[512:1024, :], slots[6](seq), 10)],
    ]
    lres = local(res_hbm.at[pl.ds(pl.multiple_of(mp * ROWS, ROWS), ROWS), :], res, 11)

    bar = pltpu.get_barrier_semaphore()
    peers = [zr, zl, xr_dev, xl_dev, core, *ys, after, before]
    for p in peers:
        pl.semaphore_signal(bar, inc=1, device_id=p, device_id_type=MESH)
    pl.semaphore_wait(bar, len(peers))

    hbm_of, buf_of, hops_of = (k_hbm, v_hbm), (kb, vb), (HOPS_A, HOPS_B)
    for i, (src, dst) in enumerate(
        ((k_hbm, kb.at[z, own_rows, :]), (v_hbm, vb.at[z, own_rows, :]), (q_hbm, qb.at[own_rows, :]))
    ):
        send(src.at[:, far_cols], dst, qx_s.at[i], qx_r.at[i], pair)
    for a in (0, 1):
        for w, to in ((RIGHT, zr), (LEFT, zl)):
            send(hbm_of[a].at[:, own_cols], buf_of[a].at[z, own_rows, :], kv1_s.at[a, w, 0], kv1_r.at[a, w, 0], to)

    def pass_half(a):
        half = buf_of[a].at[z, far_rows, :]
        arrived(half, qx_s.at[a], qx_r.at[a], pair)
        for w, to in ((RIGHT, zr), (LEFT, zl)):
            send(half, half, kv1_s.at[a, w, 1], kv1_r.at[a, w, 1], to)

    def kv_relay(a, s):
        for w, frm, to, sign in ((RIGHT, zl, zr, -1), (LEFT, zr, zl, 1)):
            if s > hops_of[a][w]:
                continue
            slot = zmod(z + sign * s)
            if s == 1:
                for half, rows in ((0, own_rows), (1, far_rows)):
                    arrived(buf_of[a].at[slot, rows, :], kv1_s.at[a, w, half], kv1_r.at[a, w, half], frm)
            else:
                arrived(buf_of[a].at[slot], kv_s.at[a, w, s - 2], kv_r.at[a, w, s - 2], frm)
            if s + 1 <= hops_of[a][w]:
                ref = buf_of[a].at[slot]
                send(ref, ref, kv_s.at[a, w, s - 1], kv_r.at[a, w, s - 1], to)

    hops_w = [HOPS_A, HOPS_B, HOPS_A, HOPS_A, HOPS_B, HOPS_A, HOPS_B]

    def x_way(p, k):
        return RIGHT if (p + k) % 2 == 0 else LEFT

    def x_send(p, k, shard):
        w = x_way(p, k)
        ref = slots[p](lo * NZ + shard)
        send(ref, ref, wx_s.at[p, k], wx_r.at[p, k], xr_dev if w == RIGHT else xl_dev)

    def begin(p):
        ref = slots[p](seq)
        for w, to in ((RIGHT, zr), (LEFT, zl)):
            send(ref, ref, wz_s.at[p, w, 0], wz_r.at[p, w, 0], to)

    def relay(p, s):
        for w, frm, to, sign in ((RIGHT, zl, zr, -1), (LEFT, zr, zl, 1)):
            if s > hops_w[p][w]:
                continue
            shard = zmod(z + sign * s)
            ref = slots[p](lo * NZ + shard)
            arrived(ref, wz_s.at[p, w, s - 1], wz_r.at[p, w, s - 1], frm)
            if s + 1 <= hops_w[p][w]:
                send(ref, ref, wz_s.at[p, w, s], wz_r.at[p, w, s], to)
            x_send(p, 7 if s == 4 else 2 * s - 1 + w, shard)

    def shard_of(k):
        return zmod(z if k == 0 else z - (k + 1) // 2 if k % 2 else z + k // 2)

    def weights_done(p, ks=range(8)):
        for k in ks:
            frm = xl_dev if x_way(p, k) == RIGHT else xr_dev
            arrived(slots[p]((1 - lo) * NZ + shard_of(k)), wx_s.at[p, k], wx_r.at[p, k], frm)

    todo = list(RELAYS)
    counts = list(PUMPS)

    def pump(n=None):
        for _ in range(min(counts.pop(0) if n is None else n, len(todo))):
            p, s = todo.pop(0)
            if s == 0:
                begin(p)
            else:
                relay(p, s)

    def need(p):
        while any(q == p for q, _ in todo):
            pump(1)
        weights_done(p)

    scale2 = math.log2(math.e) / math.sqrt(HD)

    def attend(slot, first=False, base=0, steps=3, size=256):
        def body(i, carry):
            rows = pl.ds(pl.multiple_of(base + i * size, 64), size)
            s = lax.dot_general(
                qb[rows, :], kb[slot], (((1,), (1,)), ((), ())), preferred_element_type=F32
            )
            top = jnp.max(s, axis=1, keepdims=True)
            if not first:
                old = m_s[rows, :]
                top = jnp.maximum(top, old[:, :1])
            p = jnp.exp2((s - top) * scale2)
            part = p[:, 0:128]
            for t in range(1, 6):
                part = part + p[:, t * 128 : (t + 1) * 128]
            out = jnp.dot(p.astype(BF), vb[slot], preferred_element_type=F32)
            if not first:
                shrink = jnp.exp2((old - top) * scale2)
                part = part + l_s[rows, :] * shrink
                out = out + acc[rows, :] * shrink
            m_s[rows, :] = jnp.broadcast_to(top, (size, 128))
            l_s[rows, :] = part
            acc[rows, :] = out
            return carry

        lax.fori_loop(0, steps, body, 0)

    for d in own[0]:
        d.wait()
    begin(0)
    pass_half(0)
    pass_half(1)
    for p in range(len(slots)):
        if p:
            for d in own[p]:
                d.wait()
        x_send(p, 0, z)
    lq.wait()
    lk.wait()
    lv.wait()
    arrived(qb.at[far_rows, :], qx_s.at[2], qx_r.at[2], pair)
    attend(z, first=True)
    def finish(rows, blocks):
        o = acc[rows, :] / jnp.sum(l_s[rows, :], axis=1, keepdims=True)
        ob[blocks] = o.astype(BF).reshape(8, ROWS, HD)

    far_blocks, own_blocks = pl.ds((1 - lo) * 8, 8), pl.ds(lo * 8, 8)
    for s in (1, 2, 3, 4):
        kv_relay(0, s)
        if s > 1:
            attend(zmod(z + s - 1))
        kv_relay(1, s)
        relay(0, s)
        pump()
        if s < 4:
            attend(zmod(z - s))
    attend(zmod(z + 4), base=(1 - lo) * TOK, steps=2, size=192)
    finish(far_rows, far_blocks)
    send(ob.at[far_blocks], ho.at[:, :, own_cols], o_s, o_r, pair)
    pump()
    attend(zmod(z + 4), base=lo * TOK, steps=2, size=192)
    finish(own_rows, own_blocks)
    lo_copy = local(ob.at[own_blocks], ho.at[:, :, own_cols], 12)
    for i in range(3):
        for u in range(8):
            mrow[i : i + 1, u * 128 : (u + 1) * 128] = jnp.full((1, 128), mask_ref[i, u].astype(F32))
    lres.wait()
    stream[...] = res[...].astype(F32)
    lo_copy.wait()
    pump()
    arrived(ho.at[:, :, far_cols], o_s, o_r, pair)

    def branch(n, left, weight):
        for mine in (False, True):
            side = c if mine else 1 - c
            lhs = jnp.concatenate([left[2 * b + side] for b in range(NY)], axis=0)
            for j in range(4):
                cols = slice(j * 512, (j + 1) * 512)
                prod = jnp.dot(lhs, weight[:, cols], preferred_element_type=F32).reshape(NY, ROWS, 512)
                for r in range(CHUNKS):
                    chunk = prod[:, r * 16 : (r + 1) * 16]
                    if mine:
                        ps[r, :, :, cols] = chunk
                    else:
                        xs[n, r, :, :, cols] = chunk.astype(BF)
            if not mine:
                for r in range(CHUNKS):
                    send(xs.at[n, r], xr.at[n, r], pc_s.at[n, r], pc_r.at[n, r], core)
                pump()
        for r in range(CHUNKS):
            arrived(xr.at[n, r], pc_s.at[n, r], pc_r.at[n, r], core)
            for d in (2, 1, 3):
                b = ymod(y + d)
                rs[n, r, d - 1] = (ps[r, b] + xr[n, r, b].astype(F32)).astype(BF)
                send(rs.at[n, r, d - 1], rr.at[n, r, d - 1], rx_s.at[n, r, d - 1], rx_r.at[n, r, d - 1], ys[d - 1])
        for r in range(CHUNKS):
            pump()
            rows = slice(r * 16, (r + 1) * 16)
            total = ps[r, y] + xr[n, r, y].astype(F32)
            for d in (1, 3, 2):
                arrived(rr.at[n, r, d - 1], rx_s.at[n, r, d - 1], rx_r.at[n, r, d - 1], ys[3 - d])
                total = total + rr[n, r, d - 1].astype(F32)
            new = stream[rows, :] + total
            stream[rows, :] = new
            mine = nb.at[n, mp, rows]
            nb[n, mp, rows] = layer_norm(new).astype(BF)
            for d in (2, 1, 3):
                send(mine, mine, ag_s.at[n, r, d - 1], ag_r.at[n, r, d - 1], ys[d - 1])
            send(mine, mine, agc_s.at[n, r, 0], agc_r.at[n, r, 0], core)
        for r in range(CHUNKS):
            pump()
            rows = slice(r * 16, (r + 1) * 16)
            for d in (1, 3, 2):
                got = nb.at[n, 2 * ymod(y - d) + c, rows]
                arrived(got, ag_s.at[n, r, d - 1], ag_r.at[n, r, d - 1], ys[3 - d])
                send(got, got, agc_s.at[n, r, d], agc_r.at[n, r, d], core)
        pump()
        for r in range(CHUNKS):
            rows = slice(r * 16, (r + 1) * 16)
            for d in (0, 1, 3, 2):
                arrived(nb.at[n, 2 * ymod(y - d) + 1 - c, rows], agc_s.at[n, r, d], agc_r.at[n, r, d], core)

    need(0)
    branch(0, ho, wo)

    need(1)

    def glu(rows):
        value = jnp.dot(rows, cv[:, 0:256], preferred_element_type=F32)
        gate = jnp.dot(rows, cv[:, 256:512], preferred_element_type=F32)
        return (value * jax.nn.sigmoid(gate)).astype(BF)

    edge = glu(jnp.concatenate([nb[0, 7, ROWS - 16 :, :], nb[0, 0, :16, :]], axis=0))
    gs[0] = edge[:16]
    gs[1] = edge[16:]
    send(gs.at[0], gr.at[0], h_s.at[0], h_r.at[0], after)
    send(gs.at[1], gr.at[1], h_s.at[1], h_r.at[1], before)
    gp[16 : 16 + TOK, :] = glu(nb[0].reshape(TOK, D)).astype(F32)
    pump()
    arrived(gr.at[0], h_s.at[0], h_r.at[0], before)
    arrived(gr.at[1], h_s.at[1], h_r.at[1], after)
    gp[0:16, :] = jnp.where(seq > 0, gr[0].astype(F32), 0.0)
    gp[16 + TOK :, :] = jnp.where(seq < 2 * NZ - 1, gr[1].astype(F32), 0.0)
    for r in range(8):
        sh[r] = gp[r + 1 : r + 1 + TOK + 24, :]

    def depth(i, carry):
        total = jnp.zeros((96, 256), F32)
        for t in range(TAPS):
            total = total + dk_ref[t : t + 1, :] * sh[t % 8, pl.ds(pl.multiple_of(i * 96 + t // 8 * 8, 8), 96), :]
        act[pl.ds(2 * i, 2)] = (total * jax.nn.sigmoid(total)).astype(BF).reshape(2, ROWS, 256)
        return carry

    lax.fori_loop(0, 4, depth, 0)
    pump()
    need(2)
    branch(1, act, co)

    need(3)
    need(4)

    def ffn(j, carry):
        cols = pl.ds(pl.multiple_of(j * 256, 256), 256)
        pre = jnp.dot(nb[1].reshape(TOK, D), fi[:, cols], preferred_element_type=F32)
        h = (pre * jax.nn.sigmoid(pre)).reshape(3, 128, 256) * mrow[:, cols][:, None, :]
        hid[:, :, cols] = h.astype(BF).reshape(8, ROWS, 256)
        return carry

    lax.fori_loop(0, 4, ffn, 0)
    def columns(g):
        return [
            pl.ds(pl.multiple_of((side * NZ + shard_of(k)) * 128, 128), 128)
            for side in (lo, 1 - lo) for k in (2 * g, 2 * g + 1)
        ]

    for g in range(GROUPS):
        while (5, g + 1) in todo or (6, g + 1) in todo:
            pump(1)
        for p in (5, 6):
            weights_done(p, (2 * g, 2 * g + 1))
        rhs = jnp.concatenate([fd[:, cols] for cols in columns(g)], axis=1)
        for mine in (False, True):
            side = c if mine else 1 - c
            lhs = jnp.concatenate([hid[2 * b + side] for b in range(NY)], axis=0)
            prod = jnp.dot(lhs, rhs, preferred_element_type=F32).reshape(NY, ROWS, 512)
            if mine:
                ps3[g] = prod
            else:
                xs3[g] = prod.astype(BF)
                send(xs3.at[g], xr3.at[g], pc3_s.at[g], pc3_r.at[g], core)
        arrived(xr3.at[g], pc3_s.at[g], pc3_r.at[g], core)
        for d in (2, 1, 3):
            b = ymod(y + d)
            rs3[g, d - 1] = (ps3[g, b] + xr3[g, b].astype(F32)).astype(BF)
            send(rs3.at[g, d - 1], rr3.at[g, d - 1], rx3_s.at[g, d - 1], rx3_r.at[g, d - 1], ys[d - 1])
    for g in range(GROUPS):
        total = ps3[g, y] + xr3[g, y].astype(F32)
        for d in (1, 3, 2):
            arrived(rr3.at[g, d - 1], rx3_s.at[g, d - 1], rx3_r.at[g, d - 1], ys[3 - d])
            total = total + rr3[g, d - 1].astype(F32)
        for i, cols in enumerate(columns(g)):
            stream[:, cols] += 0.5 * total[:, i * 128 : (i + 1) * 128]
    out_ref[...] = layer_norm(stream[...])
    for d in pending:
        d.wait_send()


def on_device(*args):
    dma = pltpu.SemaphoreType.DMA
    any_spec = pl.BlockSpec(memory_space=pl.ANY)
    vmem, smem = pl.BlockSpec(memory_space=pltpu.VMEM), pl.BlockSpec(memory_space=pltpu.SMEM)
    v = pltpu.VMEM
    return pl.pallas_call(
        block_kernel,
        out_shape=jax.ShapeDtypeStruct((ROWS, D), F32),
        in_specs=[any_spec] * 7 + [vmem] + [any_spec] * 3 + [smem],
        out_specs=vmem,
        scratch_shapes=[
            v((2 * TOK, HD), BF), v((NZ, 2 * TOK, HD), BF), v((NZ, 2 * TOK, HD), BF),
            v((2 * TOK, 128), F32), v((2 * TOK, 128), F32), v((2 * TOK, HD), F32),
            v((16, ROWS, HD), BF), v((8, ROWS, 256), BF),
            v((256, D), BF), v((D, 512), BF), v((256, D), BF), v((D, 1024), BF), v((1024, D), BF),
            v((ROWS, D), BF), v((ROWS, D), F32), v((CHUNKS, NY, 16, D), F32),
            v((2, CHUNKS, NY, 16, D), BF), v((2, CHUNKS, NY, 16, D), BF),
            v((2, CHUNKS, 3, 16, D), BF), v((2, CHUNKS, 3, 16, D), BF),
            v((GROUPS, NY, ROWS, 512), F32), v((GROUPS, NY, ROWS, 512), BF), v((GROUPS, NY, ROWS, 512), BF),
            v((GROUPS, 3, ROWS, 512), BF), v((GROUPS, 3, ROWS, 512), BF),
            v((2, 8, ROWS, D), BF),
            v((TOK + 32, 256), F32), v((8, TOK + 24, 256), F32), v((2, 16, 256), BF), v((2, 16, 256), BF),
            v((8, ROWS, 256), BF), v((8, ROWS, 1024), BF), v((3, 1024), F32),
            dma((13,)), dma((3,)), dma((3,)), dma((2, 2, 2)), dma((2, 2, 2)), dma((2, 2, 3)), dma((2, 2, 3)),
            dma((7, 2, 4)), dma((7, 2, 4)), dma((7, 8)), dma((7, 8)), dma(()), dma(()),
            dma((2, CHUNKS)), dma((2, CHUNKS)), dma((2, CHUNKS, 3)), dma((2, CHUNKS, 3)),
            dma((2, CHUNKS, 3)), dma((2, CHUNKS, 3)), dma((2, CHUNKS, 4)), dma((2, CHUNKS, 4)),
            dma((GROUPS,)), dma((GROUPS,)), dma((GROUPS, 3)), dma((GROUPS, 3)),
            dma((2,)), dma((2,)),
        ],
        compiler_params=pltpu.CompilerParams(
            collective_id=0, has_side_effects=True, vmem_limit_bytes=60 * 1024 * 1024
        ),
        name="block",
    )(*args)


def solution(mesh):
    in_specs = (
        P(("dp", "seq"), None),
        P(("dp", "seq"), "mp"),
        P(("dp", "seq"), "mp"),
        P(("dp", "seq"), "mp"),
        P("mp", "seq"),
        P("seq", "mp"),
        P("seq", "mp"),
        P(None, "mp"),
        P("mp", "seq"),
        P("seq", "mp"),
        P("mp", "seq"),
        P(("dp", "seq"), "mp"),
    )
    out_specs = P(("dp", "seq", "mp"), None)
    return jax.shard_map(on_device, mesh=mesh, in_specs=in_specs, out_specs=out_specs, check_vma=False)
```

```python
import math

import jax
import jax.numpy as jnp
from jax import lax
from jax.experimental import pallas as pl
from jax.experimental.pallas import tpu as pltpu
from jax.sharding import PartitionSpec as P

MESH = pl.DeviceIdType.MESH
BF, F32 = jnp.bfloat16, jnp.float32
HD = 128
NZ = 8
NY = 4
TOK = 384
ROWS = 48
D = 2048
EPS = 1e-05
TAPS = 31
RIGHT, LEFT = 0, 1
HOPS_A, HOPS_B = (4, 3), (3, 4)
CHUNKS, GROUPS = ROWS // 16, 4
RELAYS = [
    (1, 0), (2, 0), (4, 0), (1, 1), (2, 1), (3, 0), (1, 2), (2, 2), (4, 1), (1, 3), (5, 0), (2, 3),
    (3, 1), (1, 4), (2, 4), (6, 0), (5, 1), (3, 2), (6, 1), (4, 2), (3, 3), (6, 2), (4, 3), (5, 2),
    (3, 4), (4, 4), (6, 3), (5, 3), (6, 4), (5, 4),
]
PUMPS = [
    1, 0, 0, 0, 0, 0, 3, 0, 0, 2, 0, 1, 4, 2, 0, 0, 0, 1, 0, 3, 1, 0, 0, 2,
    0, 0, 4, 1, 0, 0, 2, 0, 1, 0, 2, 0, 0,
]


def layer_norm(x):
    mean = jnp.mean(x, axis=-1, keepdims=True)
    cen = x - mean
    var = jnp.mean(cen * cen, axis=-1, keepdims=True)
    return cen * lax.rsqrt(var + EPS)


def block_kernel(
    res_hbm, q_hbm, k_hbm, v_hbm, wo_hbm, cval_hbm, cgate_hbm, dk_ref, co_hbm, fi_hbm, fd_hbm, mask_ref,
    out_ref,
    qb, kb, vb, m_s, l_s, acc, ob, ho, wo, cv, co, fi, fd, res, stream, ps, xs, xr, rs, rr, ps3, xs3, xr3, rs3, rr3, nb,
    gp, sh, gs, gr, act, hid, mrow,
    loc, qx_s, qx_r, kv1_s, kv1_r, kv_s, kv_r, wz_s, wz_r, wx_s, wx_r, o_s, o_r,
    pc_s, pc_r, rx_s, rx_r, ag_s, ag_r, agc_s, agc_r, pc3_s, pc3_r, rx3_s, rx3_r, h_s, h_r,
):
    seq, mp, dp = lax.axis_index("seq"), lax.axis_index("mp"), lax.axis_index("dp")
    lo, z = lax.div(seq, NZ), lax.rem(seq, NZ)
    y, c = lax.div(mp, 2), lax.rem(mp, 2)

    def zmod(a):
        return lax.rem(a + 2 * NZ, NZ)

    def ymod(a):
        return lax.rem(a + 2 * NY, NY)

    def dev(s, m, d):
        return {"seq": s, "mp": m, "dp": d}

    zr = dev(lo * NZ + zmod(z + 1), mp, dp)
    zl = dev(lo * NZ + zmod(z - 1), mp, dp)
    other_seq = (1 - lo) * NZ + z
    xr_dev = dev(other_seq, mp, lax.rem(dp + lo, 2))
    xl_dev = dev(other_seq, mp, lax.rem(dp + 1 - lo, 2))
    pair = dev(other_seq, mp, dp)
    core = dev(seq, 2 * y + 1 - c, dp)
    yr, yl = dev(seq, 2 * ymod(y + 1) + c, dp), dev(seq, 2 * ymod(y - 1) + c, dp)
    yo = dev(seq, 2 * ymod(y + 2) + c, dp)
    after = dev(lax.rem(seq + 1, 2 * NZ), mp, dp)
    before = dev(lax.rem(seq + 2 * NZ - 1, 2 * NZ), mp, dp)

    pending = []

    def send(src, dst, ssem, rsem, to):
        d = pltpu.make_async_remote_copy(
            src_ref=src, dst_ref=dst, send_sem=ssem, recv_sem=rsem, device_id=to, device_id_type=MESH
        )
        d.start()
        pending.append(d)

    def arrived(dst, ssem, rsem, frm):
        pltpu.make_async_remote_copy(
            src_ref=dst, dst_ref=dst, send_sem=ssem, recv_sem=rsem, device_id=frm, device_id_type=MESH
        ).wait_recv()

    def local(src, dst, i):
        d = pltpu.make_async_copy(src, dst, loc.at[i])
        d.start()
        return d

    own_cols, far_cols = pl.ds(pl.multiple_of(lo * HD, HD), HD), pl.ds(pl.multiple_of((1 - lo) * HD, HD), HD)
    own_rows = pl.ds(pl.multiple_of(lo * TOK, TOK), TOK)
    far_rows = pl.ds(pl.multiple_of((1 - lo) * TOK, TOK), TOK)

    def col_slot(ref):
        return lambda j: ref.at[:, pl.ds(pl.multiple_of(j * 128, 128), 128)]

    def row_slot(ref):
        return lambda j: ref.at[pl.ds(pl.multiple_of(j * 128, 128), 128), :]

    slots = [
        col_slot(wo), row_slot(cv), col_slot(co), row_slot(fi.at[:, 0:512]), row_slot(fi.at[:, 512:1024]),
        col_slot(fd.at[0:512, :]), col_slot(fd.at[512:1024, :]),
    ]
    my_rows = pl.ds(pl.multiple_of(seq * 128, 128), 128)
    lk = local(k_hbm.at[:, own_cols], kb.at[z, own_rows, :], 0)
    lv = local(v_hbm.at[:, own_cols], vb.at[z, own_rows, :], 1)
    lq = local(q_hbm.at[:, own_cols], qb.at[own_rows, :], 2)
    own = [
        [local(wo_hbm, slots[0](seq), 3)],
        [local(cval_hbm, cv.at[my_rows, 0:256], 4), local(cgate_hbm, cv.at[my_rows, 256:512], 5)],
        [local(co_hbm, slots[2](seq), 6)],
        [local(fi_hbm.at[:, 0:512], slots[3](seq), 7)],
        [local(fi_hbm.at[:, 512:1024], slots[4](seq), 8)],
        [local(fd_hbm.at[0:512, :], slots[5](seq), 9)],
        [local(fd_hbm.at[512:1024, :], slots[6](seq), 10)],
    ]
    lres = local(res_hbm.at[pl.ds(pl.multiple_of(mp * ROWS, ROWS), ROWS), :], res, 11)

    bar = pltpu.get_barrier_semaphore()
    peers = [zr, zl, xr_dev, xl_dev, core, yr, yl, yo, after, before]
    for p in peers:
        pl.semaphore_signal(bar, inc=1, device_id=p, device_id_type=MESH)
    pl.semaphore_wait(bar, len(peers))

    hbm_of, buf_of, hops_of = (k_hbm, v_hbm), (kb, vb), (HOPS_A, HOPS_B)
    for i, (src, dst) in enumerate(
        ((k_hbm, kb.at[z, own_rows, :]), (v_hbm, vb.at[z, own_rows, :]), (q_hbm, qb.at[own_rows, :]))
    ):
        send(src.at[:, far_cols], dst, qx_s.at[i], qx_r.at[i], pair)
    for a in (0, 1):
        for w, to in ((RIGHT, zr), (LEFT, zl)):
            send(hbm_of[a].at[:, own_cols], buf_of[a].at[z, own_rows, :], kv1_s.at[a, w, 0], kv1_r.at[a, w, 0], to)

    def pass_half(a):
        half = buf_of[a].at[z, far_rows, :]
        arrived(half, qx_s.at[a], qx_r.at[a], pair)
        for w, to in ((RIGHT, zr), (LEFT, zl)):
            send(half, half, kv1_s.at[a, w, 1], kv1_r.at[a, w, 1], to)

    def kv_relay(a, s):
        for w, frm, to, sign in ((RIGHT, zl, zr, -1), (LEFT, zr, zl, 1)):
            if s > hops_of[a][w]:
                continue
            slot = zmod(z + sign * s)
            if s == 1:
                for half, rows in ((0, own_rows), (1, far_rows)):
                    arrived(buf_of[a].at[slot, rows, :], kv1_s.at[a, w, half], kv1_r.at[a, w, half], frm)
            else:
                arrived(buf_of[a].at[slot], kv_s.at[a, w, s - 2], kv_r.at[a, w, s - 2], frm)
            if s + 1 <= hops_of[a][w]:
                ref = buf_of[a].at[slot]
                send(ref, ref, kv_s.at[a, w, s - 1], kv_r.at[a, w, s - 1], to)

    hops_w = [HOPS_A, HOPS_B, HOPS_A, HOPS_A, HOPS_B, HOPS_A, HOPS_B]

    def x_way(p, k):
        return RIGHT if (p + k) % 2 == 0 else LEFT

    def x_send(p, k, shard):
        w = x_way(p, k)
        ref = slots[p](lo * NZ + shard)
        send(ref, ref, wx_s.at[p, k], wx_r.at[p, k], xr_dev if w == RIGHT else xl_dev)

    def begin(p):
        ref = slots[p](seq)
        for w, to in ((RIGHT, zr), (LEFT, zl)):
            send(ref, ref, wz_s.at[p, w, 0], wz_r.at[p, w, 0], to)

    def relay(p, s):
        for w, frm, to, sign in ((RIGHT, zl, zr, -1), (LEFT, zr, zl, 1)):
            if s > hops_w[p][w]:
                continue
            shard = zmod(z + sign * s)
            ref = slots[p](lo * NZ + shard)
            arrived(ref, wz_s.at[p, w, s - 1], wz_r.at[p, w, s - 1], frm)
            if s + 1 <= hops_w[p][w]:
                send(ref, ref, wz_s.at[p, w, s], wz_r.at[p, w, s], to)
            x_send(p, 7 if s == 4 else 2 * s - 1 + w, shard)

    def shard_of(k):
        return zmod(z if k == 0 else z - (k + 1) // 2 if k % 2 else z + k // 2)

    def weights_done(p, ks=range(8)):
        for k in ks:
            frm = xl_dev if x_way(p, k) == RIGHT else xr_dev
            arrived(slots[p]((1 - lo) * NZ + shard_of(k)), wx_s.at[p, k], wx_r.at[p, k], frm)

    todo = list(RELAYS)
    counts = list(PUMPS)

    def pump(n=None):
        for _ in range(min(counts.pop(0) if n is None else n, len(todo))):
            p, s = todo.pop(0)
            if s == 0:
                begin(p)
            else:
                relay(p, s)

    def need(p):
        while any(q == p for q, _ in todo):
            pump(1)
        weights_done(p)

    scale2 = math.log2(math.e) / math.sqrt(HD)

    def attend(slot, first=False, base=0, steps=2, size=384):
        for i in range(steps):
            rows = pl.ds(pl.multiple_of(base + i * size, 64), size)
            s = lax.dot_general(
                qb[rows, :], kb[slot], (((1,), (1,)), ((), ())), preferred_element_type=F32
            )
            top = jnp.max(s, axis=1, keepdims=True)
            if not first:
                old = m_s[rows, :]
                top = jnp.maximum(top, old[:, :1])
            p = jnp.exp2((s - top) * scale2)
            part = p[:, 0:128]
            for t in range(1, 6):
                part = part + p[:, t * 128 : (t + 1) * 128]
            out = jnp.dot(p.astype(BF), vb[slot], preferred_element_type=F32)
            if not first:
                shrink = jnp.exp2((old - top) * scale2)
                part = part + l_s[rows, :] * shrink
                out = out + acc[rows, :] * shrink
            m_s[rows, :] = jnp.broadcast_to(top, (size, 128))
            l_s[rows, :] = part
            acc[rows, :] = out

    for d in own[0]:
        d.wait()
    begin(0)
    pass_half(0)
    pass_half(1)
    for p in range(len(slots)):
        if p:
            for d in own[p]:
                d.wait()
        x_send(p, 0, z)
    pump()
    lq.wait()
    lk.wait()
    lv.wait()
    arrived(qb.at[far_rows, :], qx_s.at[2], qx_r.at[2], pair)
    attend(z, first=True)
    def finish(rows, blocks):
        o = acc[rows, :] / jnp.sum(l_s[rows, :], axis=1, keepdims=True)
        ob[blocks] = o.astype(BF).reshape(8, ROWS, HD)

    far_blocks, own_blocks = pl.ds((1 - lo) * 8, 8), pl.ds(lo * 8, 8)
    for s in (1, 2, 3, 4):
        kv_relay(0, s)
        pump()
        if s > 1:
            attend(zmod(z + s - 1))
        kv_relay(1, s)
        relay(0, s)
        pump()
        if s < 4:
            attend(zmod(z - s))
    attend(zmod(z + 4), base=(1 - lo) * TOK, steps=2, size=192)
    finish(far_rows, far_blocks)
    send(ob.at[far_blocks], ho.at[:, :, own_cols], o_s, o_r, pair)
    pump()
    attend(zmod(z + 4), base=lo * TOK, steps=2, size=192)
    finish(own_rows, own_blocks)
    lo_copy = local(ob.at[own_blocks], ho.at[:, :, own_cols], 12)
    for i in range(3):
        for u in range(8):
            mrow[i : i + 1, u * 128 : (u + 1) * 128] = jnp.full((1, 128), mask_ref[i, u].astype(F32))
    lres.wait()
    stream[...] = res[...].astype(F32)
    lo_copy.wait()
    pump()
    arrived(ho.at[:, :, far_cols], o_s, o_r, pair)

    class Scatter:
        def __init__(self, part, out, got, ssem, rsem):
            self.part, self.out, self.got, self.ssem, self.rsem = part, out, got, ssem, rsem

        def put(self, i, value):
            self.out[i] = value.astype(BF)
            send(self.out.at[i], self.got.at[i], self.ssem.at[i], self.rsem.at[i], yl if i % 2 else yr)

        def take(self, i):
            arrived(self.got.at[i], self.ssem.at[i], self.rsem.at[i], yr if i % 2 else yl)
            return self.got[i].astype(F32)

        def first(self):
            right, left, far = ymod(y + 1), ymod(y - 1), ymod(y + 2)
            self.put(0, self.part(far, 0))
            self.put(1, self.part(far, 1))
            self.put(2, self.part(right, 1))
            self.put(3, self.part(left, 0))

        def direct(self):
            right, left, far = ymod(y + 1), ymod(y - 1), ymod(y + 2)
            for i, (b, to) in enumerate(((far, yo), (far, yo), (right, yr), (left, yl), (right, yr), (left, yl))):
                self.out[i] = self.part(b, (0, 1, 1, 0, 0, 1)[i]).astype(BF)
                send(self.out.at[i], self.got.at[i], self.ssem.at[i], self.rsem.at[i], to)

        def direct_total(self):
            halves = [self.part(y, 0), self.part(y, 1)]
            for i, frm in ((3, yr), (4, yl), (2, yl), (5, yr), (0, yo), (1, yo)):
                arrived(self.got.at[i], self.ssem.at[i], self.rsem.at[i], frm)
                halves[(0, 1, 1, 0, 0, 1)[i]] += self.got[i].astype(F32)
            return jnp.concatenate(halves, axis=1)

        def second(self):
            self.put(4, self.part(ymod(y + 1), 0) + self.take(0))
            self.put(5, self.part(ymod(y - 1), 1) + self.take(1))

        def total(self):
            low = self.part(y, 0) + self.take(3) + self.take(4)
            high = self.part(y, 1) + self.take(2) + self.take(5)
            return jnp.concatenate([low, high], axis=1)

    def branch(n, left, weight):
        for mine in (False, True):
            side = c if mine else 1 - c
            lhs = jnp.concatenate([left[2 * b + side] for b in range(NY)], axis=0)
            for j in range(4):
                cols = slice(j * 512, (j + 1) * 512)
                prod = jnp.dot(lhs, weight[:, cols], preferred_element_type=F32).reshape(NY, ROWS, 512)
                for r in range(CHUNKS):
                    chunk = prod[:, r * 16 : (r + 1) * 16]
                    if mine:
                        ps[r, :, :, cols] = chunk
                    else:
                        xs[n, r, :, :, cols] = chunk.astype(BF)
            if not mine:
                for r in range(CHUNKS):
                    send(xs.at[n, r], xr.at[n, r], pc_s.at[n, r], pc_r.at[n, r], core)
                pump()
        half = D // 2

        def part_of(r):
            def part(b, h):
                cols = slice(h * half, (h + 1) * half)
                return ps[r, b, :, cols] + xr[n, r, b, :, cols].astype(F32)

            return part

        chunks = [
            Scatter(part_of(r), rs.at[n, r], rr.at[n, r], rx_s.at[n, r], rx_r.at[n, r]) for r in range(CHUNKS)
        ]
        for r in range(CHUNKS):
            arrived(xr.at[n, r], pc_s.at[n, r], pc_r.at[n, r], core)
            if r:
                chunks[r].first()
            else:
                chunks[r].direct()
        for r in range(1, CHUNKS):
            pump()
            chunks[r].second()
        for r in range(CHUNKS):
            pump()
            rows = slice(r * 16, (r + 1) * 16)
            new = stream[rows, :] + (chunks[r].total() if r else chunks[r].direct_total())
            stream[rows, :] = new
            nb[n, mp, rows] = layer_norm(new).astype(BF)
            mine = nb.at[n, mp, rows]
            send(mine, mine, ag_s.at[n, r, 0], ag_r.at[n, r, 0], yr)
            send(mine, mine, ag_s.at[n, r, 1], ag_r.at[n, r, 1], yl)
            if r == CHUNKS - 1:
                send(mine, mine, ag_s.at[n, r, 2], ag_r.at[n, r, 2], yo)
            send(mine, mine, agc_s.at[n, r, 0], agc_r.at[n, r, 0], core)
        for r in range(CHUNKS):
            pump()
            rows = slice(r * 16, (r + 1) * 16)
            for i, (d, frm, to) in enumerate(((1, yl, yr), (3, yr, yl))):
                b = 2 * ymod(y - d) + c
                got, part = nb.at[n, b, rows], nb.at[n, b, rows, i * half : (i + 1) * half]
                arrived(got, ag_s.at[n, r, i], ag_r.at[n, r, i], frm)
                if r < CHUNKS - 1:
                    send(part, part, ag_s.at[n, r, 2 + i], ag_r.at[n, r, 2 + i], to)
                send(got, got, agc_s.at[n, r, d], agc_r.at[n, r, d], core)
        for r in range(CHUNKS):
            pump()
            rows = slice(r * 16, (r + 1) * 16)
            b = 2 * ymod(y + 2) + c
            if r < CHUNKS - 1:
                for i, frm in enumerate((yl, yr)):
                    part = nb.at[n, b, rows, i * half : (i + 1) * half]
                    arrived(part, ag_s.at[n, r, 2 + i], ag_r.at[n, r, 2 + i], frm)
            else:
                arrived(nb.at[n, b, rows], ag_s.at[n, r, 2], ag_r.at[n, r, 2], yo)
            send(nb.at[n, b, rows], nb.at[n, b, rows], agc_s.at[n, r, 2], agc_r.at[n, r, 2], core)
        for r in range(CHUNKS):
            rows = slice(r * 16, (r + 1) * 16)
            for d in (0, 1, 3, 2):
                arrived(nb.at[n, 2 * ymod(y - d) + 1 - c, rows], agc_s.at[n, r, d], agc_r.at[n, r, d], core)

    need(0)
    branch(0, ho, wo)

    need(1)

    def glu(rows):
        value = jnp.dot(rows, cv[:, 0:256], preferred_element_type=F32)
        gate = jnp.dot(rows, cv[:, 256:512], preferred_element_type=F32)
        return (value * jax.nn.sigmoid(gate)).astype(BF)

    edge = glu(jnp.concatenate([nb[0, 7, ROWS - 16 :, :], nb[0, 0, :16, :]], axis=0))
    gs[0] = edge[:16]
    gs[1] = edge[16:]
    send(gs.at[0], gr.at[0], h_s.at[0], h_r.at[0], after)
    send(gs.at[1], gr.at[1], h_s.at[1], h_r.at[1], before)
    gp[16 : 16 + TOK, :] = glu(nb[0].reshape(TOK, D)).astype(F32)
    pump()
    arrived(gr.at[0], h_s.at[0], h_r.at[0], before)
    arrived(gr.at[1], h_s.at[1], h_r.at[1], after)
    gp[0:16, :] = jnp.where(seq > 0, gr[0].astype(F32), 0.0)
    gp[16 + TOK :, :] = jnp.where(seq < 2 * NZ - 1, gr[1].astype(F32), 0.0)
    for r in range(8):
        sh[r] = gp[r + 1 : r + 1 + TOK + 24, :]

    def depth(i, carry):
        total = jnp.zeros((96, 256), F32)
        for t in range(TAPS):
            total = total + dk_ref[t : t + 1, :] * sh[t % 8, pl.ds(pl.multiple_of(i * 96 + t // 8 * 8, 8), 96), :]
        act[pl.ds(2 * i, 2)] = (total * jax.nn.sigmoid(total)).astype(BF).reshape(2, ROWS, 256)
        return carry

    lax.fori_loop(0, 4, depth, 0)
    pump()
    need(2)
    branch(1, act, co)

    need(3)
    need(4)

    def ffn(j, carry):
        cols = pl.ds(pl.multiple_of(j * 256, 256), 256)
        pre = jnp.dot(nb[1].reshape(TOK, D), fi[:, cols], preferred_element_type=F32)
        h = (pre * jax.nn.sigmoid(pre)).reshape(3, 128, 256) * mrow[:, cols][:, None, :]
        hid[:, :, cols] = h.astype(BF).reshape(8, ROWS, 256)
        return carry

    lax.fori_loop(0, 4, ffn, 0)
    def columns(g):
        return [
            pl.ds(pl.multiple_of((side * NZ + shard_of(k)) * 128, 128), 128)
            for side in (lo, 1 - lo) for k in (2 * g, 2 * g + 1)
        ]

    def part_of(g):
        return lambda b, h: ps3[g, b, :, h * 256 : (h + 1) * 256] + xr3[g, b, :, h * 256 : (h + 1) * 256].astype(F32)

    groups = [Scatter(part_of(g), rs3.at[g], rr3.at[g], rx3_s.at[g], rx3_r.at[g]) for g in range(GROUPS)]
    def open_group(g):
        arrived(xr3.at[g], pc3_s.at[g], pc3_r.at[g], core)
        groups[g].first()

    for g in range(GROUPS):
        while (5, g + 1) in todo or (6, g + 1) in todo:
            pump(1)
        for p in (5, 6):
            weights_done(p, (2 * g, 2 * g + 1))
        rhs = jnp.concatenate([fd[:, cols] for cols in columns(g)], axis=1)
        for mine in (False, True):
            side = c if mine else 1 - c
            lhs = jnp.concatenate([hid[2 * b + side] for b in range(NY)], axis=0)
            prod = jnp.dot(lhs, rhs, preferred_element_type=F32).reshape(NY, ROWS, 512)
            if mine:
                ps3[g] = prod
            else:
                xs3[g] = prod.astype(BF)
                send(xs3.at[g], xr3.at[g], pc3_s.at[g], pc3_r.at[g], core)
        if g:
            open_group(g - 1)
        if g > 1:
            groups[g - 2].second()
    arrived(xr3.at[GROUPS - 1], pc3_s.at[GROUPS - 1], pc3_r.at[GROUPS - 1], core)
    groups[GROUPS - 1].direct()
    groups[GROUPS - 2].second()
    for g in range(GROUPS):
        total = groups[g].total() if g < GROUPS - 1 else groups[g].direct_total()
        for i, cols in enumerate(columns(g)):
            stream[:, cols] += 0.5 * total[:, i * 128 : (i + 1) * 128]
    out_ref[...] = layer_norm(stream[...])
    for d in pending:
        d.wait_send()


def on_device(*args):
    dma = pltpu.SemaphoreType.DMA
    any_spec = pl.BlockSpec(memory_space=pl.ANY)
    vmem, smem = pl.BlockSpec(memory_space=pltpu.VMEM), pl.BlockSpec(memory_space=pltpu.SMEM)
    v = pltpu.VMEM
    return pl.pallas_call(
        block_kernel,
        out_shape=jax.ShapeDtypeStruct((ROWS, D), F32),
        in_specs=[any_spec] * 7 + [vmem] + [any_spec] * 3 + [smem],
        out_specs=vmem,
        scratch_shapes=[
            v((2 * TOK, HD), BF), v((NZ, 2 * TOK, HD), BF), v((NZ, 2 * TOK, HD), BF),
            v((2 * TOK, 128), F32), v((2 * TOK, 128), F32), v((2 * TOK, HD), F32),
            v((16, ROWS, HD), BF), v((8, ROWS, 256), BF),
            v((256, D), BF), v((D, 512), BF), v((256, D), BF), v((D, 1024), BF), v((1024, D), BF),
            v((ROWS, D), BF), v((ROWS, D), F32), v((CHUNKS, NY, 16, D), F32),
            v((2, CHUNKS, NY, 16, D), BF), v((2, CHUNKS, NY, 16, D), BF),
            v((2, CHUNKS, 6, 16, D // 2), BF), v((2, CHUNKS, 6, 16, D // 2), BF),
            v((GROUPS, NY, ROWS, 512), F32), v((GROUPS, NY, ROWS, 512), BF), v((GROUPS, NY, ROWS, 512), BF),
            v((GROUPS, 6, ROWS, 256), BF), v((GROUPS, 6, ROWS, 256), BF),
            v((2, 8, ROWS, D), BF),
            v((TOK + 32, 256), F32), v((8, TOK + 24, 256), F32), v((2, 16, 256), BF), v((2, 16, 256), BF),
            v((8, ROWS, 256), BF), v((8, ROWS, 1024), BF), v((3, 1024), F32),
            dma((13,)), dma((3,)), dma((3,)), dma((2, 2, 2)), dma((2, 2, 2)), dma((2, 2, 3)), dma((2, 2, 3)),
            dma((7, 2, 4)), dma((7, 2, 4)), dma((7, 8)), dma((7, 8)), dma(()), dma(()),
            dma((2, CHUNKS)), dma((2, CHUNKS)), dma((2, CHUNKS, 6)), dma((2, CHUNKS, 6)),
            dma((2, CHUNKS, 4)), dma((2, CHUNKS, 4)), dma((2, CHUNKS, 4)), dma((2, CHUNKS, 4)),
            dma((GROUPS,)), dma((GROUPS,)), dma((GROUPS, 6)), dma((GROUPS, 6)),
            dma((2,)), dma((2,)),
        ],
        compiler_params=pltpu.CompilerParams(
            collective_id=0, has_side_effects=True, vmem_limit_bytes=60 * 1024 * 1024
        ),
        name="block",
    )(*args)


def solution(mesh):
    in_specs = (
        P(("dp", "seq"), None),
        P(("dp", "seq"), "mp"),
        P(("dp", "seq"), "mp"),
        P(("dp", "seq"), "mp"),
        P("mp", "seq"),
        P("seq", "mp"),
        P("seq", "mp"),
        P(None, "mp"),
        P("mp", "seq"),
        P("seq", "mp"),
        P("mp", "seq"),
        P(("dp", "seq"), "mp"),
    )
    out_specs = P(("dp", "seq", "mp"), None)
    return jax.shard_map(on_device, mesh=mesh, in_specs=in_specs, out_specs=out_specs, check_vma=False)
```

```python
import math

import jax
import jax.numpy as jnp
from jax import lax
from jax.experimental import pallas as pl
from jax.experimental.pallas import tpu as pltpu
from jax.sharding import PartitionSpec as P

MESH = pl.DeviceIdType.MESH
BF, F32 = jnp.bfloat16, jnp.float32
HD = 128
NZ = 8
NY = 4
TOK = 384
ROWS = 48
D = 2048
EPS = 1e-05
TAPS = 31
RIGHT, LEFT = 0, 1
HOPS_A, HOPS_B = (4, 3), (3, 4)
CHUNKS, GROUPS = ROWS // 16, 4
RELAYS = [
    (1, 0), (2, 0), (4, 0), (1, 1), (2, 1), (3, 0), (1, 2), (2, 2), (4, 1), (1, 3), (5, 0), (2, 3),
    (3, 1), (1, 4), (2, 4), (6, 0), (5, 1), (3, 2), (6, 1), (4, 2), (3, 3), (6, 2), (4, 3), (5, 2),
    (3, 4), (4, 4), (6, 3), (5, 3), (6, 4), (5, 4),
]
PUMPS = [
    1, 0, 0, 0, 0, 0, 3, 0, 0, 2, 0, 1, 4, 2, 0, 0, 0, 1, 0, 3, 1, 0, 0, 2,
    0, 0, 4, 1, 0, 0, 2, 0, 1, 0, 2, 0, 0,
]


def layer_norm(x):
    mean = jnp.mean(x, axis=-1, keepdims=True)
    cen = x - mean
    var = jnp.mean(cen * cen, axis=-1, keepdims=True)
    return cen * lax.rsqrt(var + EPS)


def block_kernel(
    res_hbm, q_hbm, k_hbm, v_hbm, wo_hbm, cval_hbm, cgate_hbm, dk_ref, co_hbm, fi_hbm, fd_hbm, mask_ref,
    out_ref,
    qb, kb, vb, m_s, l_s, acc, ob, ho, wo, cv, co, fi, fd, res, stream, ps, xs, xr, rs, rr, ps3, xs3, xr3, rs3, rr3, nb,
    gp, sh, gs, gr, act, hid, mrow,
    loc, qx_s, qx_r, kv1_s, kv1_r, kv_s, kv_r, wz_s, wz_r, wx_s, wx_r, o_s, o_r,
    pc_s, pc_r, rx_s, rx_r, ag_s, ag_r, agc_s, agc_r, pc3_s, pc3_r, rx3_s, rx3_r, h_s, h_r,
):
    seq, mp, dp = lax.axis_index("seq"), lax.axis_index("mp"), lax.axis_index("dp")
    lo, z = lax.div(seq, NZ), lax.rem(seq, NZ)
    y, c = lax.div(mp, 2), lax.rem(mp, 2)

    def zmod(a):
        return lax.rem(a + 2 * NZ, NZ)

    def ymod(a):
        return lax.rem(a + 2 * NY, NY)

    def dev(s, m, d):
        return {"seq": s, "mp": m, "dp": d}

    zr = dev(lo * NZ + zmod(z + 1), mp, dp)
    zl = dev(lo * NZ + zmod(z - 1), mp, dp)
    other_seq = (1 - lo) * NZ + z
    xr_dev = dev(other_seq, mp, lax.rem(dp + lo, 2))
    xl_dev = dev(other_seq, mp, lax.rem(dp + 1 - lo, 2))
    pair = dev(other_seq, mp, dp)
    core = dev(seq, 2 * y + 1 - c, dp)
    yr, yl = dev(seq, 2 * ymod(y + 1) + c, dp), dev(seq, 2 * ymod(y - 1) + c, dp)
    yo = dev(seq, 2 * ymod(y + 2) + c, dp)
    after = dev(lax.rem(seq + 1, 2 * NZ), mp, dp)
    before = dev(lax.rem(seq + 2 * NZ - 1, 2 * NZ), mp, dp)

    pending = []

    def send(src, dst, ssem, rsem, to):
        d = pltpu.make_async_remote_copy(
            src_ref=src, dst_ref=dst, send_sem=ssem, recv_sem=rsem, device_id=to, device_id_type=MESH
        )
        d.start()
        pending.append(d)

    def arrived(dst, ssem, rsem, frm):
        pltpu.make_async_remote_copy(
            src_ref=dst, dst_ref=dst, send_sem=ssem, recv_sem=rsem, device_id=frm, device_id_type=MESH
        ).wait_recv()

    def local(src, dst, i):
        d = pltpu.make_async_copy(src, dst, loc.at[i])
        d.start()
        return d

    own_cols, far_cols = pl.ds(pl.multiple_of(lo * HD, HD), HD), pl.ds(pl.multiple_of((1 - lo) * HD, HD), HD)
    own_rows = pl.ds(pl.multiple_of(lo * TOK, TOK), TOK)
    far_rows = pl.ds(pl.multiple_of((1 - lo) * TOK, TOK), TOK)

    def col_slot(ref):
        return lambda j: ref.at[:, pl.ds(pl.multiple_of(j * 128, 128), 128)]

    def row_slot(ref):
        return lambda j: ref.at[pl.ds(pl.multiple_of(j * 128, 128), 128), :]

    slots = [
        col_slot(wo), row_slot(cv), col_slot(co), row_slot(fi.at[:, 0:512]), row_slot(fi.at[:, 512:1024]),
        col_slot(fd.at[0:512, :]), col_slot(fd.at[512:1024, :]),
    ]
    my_rows = pl.ds(pl.multiple_of(seq * 128, 128), 128)
    lk = local(k_hbm.at[:, own_cols], kb.at[z, own_rows, :], 0)
    lv = local(v_hbm.at[:, own_cols], vb.at[z, own_rows, :], 1)
    lq = local(q_hbm.at[:, own_cols], qb.at[own_rows, :], 2)
    own = [
        [local(wo_hbm, slots[0](seq), 3)],
        [local(cval_hbm, cv.at[my_rows, 0:256], 4), local(cgate_hbm, cv.at[my_rows, 256:512], 5)],
        [local(co_hbm, slots[2](seq), 6)],
        [local(fi_hbm.at[:, 0:512], slots[3](seq), 7)],
        [local(fi_hbm.at[:, 512:1024], slots[4](seq), 8)],
        [local(fd_hbm.at[0:512, :], slots[5](seq), 9)],
        [local(fd_hbm.at[512:1024, :], slots[6](seq), 10)],
    ]
    lres = local(res_hbm.at[pl.ds(pl.multiple_of(mp * ROWS, ROWS), ROWS), :], res, 11)

    bar = pltpu.get_barrier_semaphore()
    peers = [zr, zl, xr_dev, xl_dev, core, yr, yl, yo, after, before]
    for p in peers:
        pl.semaphore_signal(bar, inc=1, device_id=p, device_id_type=MESH)
    pl.semaphore_wait(bar, len(peers))

    hbm_of, buf_of, hops_of = (k_hbm, v_hbm), (kb, vb), (HOPS_A, HOPS_B)
    for i, (src, dst) in enumerate(
        ((k_hbm, kb.at[z, own_rows, :]), (v_hbm, vb.at[z, own_rows, :]), (q_hbm, qb.at[own_rows, :]))
    ):
        send(src.at[:, far_cols], dst, qx_s.at[i], qx_r.at[i], pair)
    for a in (0, 1):
        for w, to in ((RIGHT, zr), (LEFT, zl)):
            send(hbm_of[a].at[:, own_cols], buf_of[a].at[z, own_rows, :], kv1_s.at[a, w, 0], kv1_r.at[a, w, 0], to)

    def pass_half(a):
        half = buf_of[a].at[z, far_rows, :]
        arrived(half, qx_s.at[a], qx_r.at[a], pair)
        for w, to in ((RIGHT, zr), (LEFT, zl)):
            send(half, half, kv1_s.at[a, w, 1], kv1_r.at[a, w, 1], to)

    def kv_relay(a, s):
        for w, frm, to, sign in ((RIGHT, zl, zr, -1), (LEFT, zr, zl, 1)):
            if s > hops_of[a][w]:
                continue
            slot = zmod(z + sign * s)
            if s == 1:
                for half, rows in ((0, own_rows), (1, far_rows)):
                    arrived(buf_of[a].at[slot, rows, :], kv1_s.at[a, w, half], kv1_r.at[a, w, half], frm)
            else:
                arrived(buf_of[a].at[slot], kv_s.at[a, w, s - 2], kv_r.at[a, w, s - 2], frm)
            if s + 1 <= hops_of[a][w]:
                ref = buf_of[a].at[slot]
                send(ref, ref, kv_s.at[a, w, s - 1], kv_r.at[a, w, s - 1], to)

    hops_w = [HOPS_A, HOPS_B, HOPS_A, HOPS_A, HOPS_B, HOPS_A, HOPS_B]

    def x_way(p, k):
        return RIGHT if (p + k) % 2 == 0 else LEFT

    def x_send(p, k, shard):
        w = x_way(p, k)
        ref = slots[p](lo * NZ + shard)
        send(ref, ref, wx_s.at[p, k], wx_r.at[p, k], xr_dev if w == RIGHT else xl_dev)

    def begin(p):
        ref = slots[p](seq)
        for w, to in ((RIGHT, zr), (LEFT, zl)):
            send(ref, ref, wz_s.at[p, w, 0], wz_r.at[p, w, 0], to)

    def relay(p, s):
        for w, frm, to, sign in ((RIGHT, zl, zr, -1), (LEFT, zr, zl, 1)):
            if s > hops_w[p][w]:
                continue
            shard = zmod(z + sign * s)
            ref = slots[p](lo * NZ + shard)
            arrived(ref, wz_s.at[p, w, s - 1], wz_r.at[p, w, s - 1], frm)
            if s + 1 <= hops_w[p][w]:
                send(ref, ref, wz_s.at[p, w, s], wz_r.at[p, w, s], to)
            x_send(p, 7 if s == 4 else 2 * s - 1 + w, shard)

    def shard_of(k):
        return zmod(z if k == 0 else z - (k + 1) // 2 if k % 2 else z + k // 2)

    def weights_done(p, ks=range(8)):
        for k in ks:
            frm = xl_dev if x_way(p, k) == RIGHT else xr_dev
            arrived(slots[p]((1 - lo) * NZ + shard_of(k)), wx_s.at[p, k], wx_r.at[p, k], frm)

    todo = list(RELAYS)
    counts = list(PUMPS)

    def pump(n=None):
        for _ in range(min(counts.pop(0) if n is None else n, len(todo))):
            p, s = todo.pop(0)
            if s == 0:
                begin(p)
            else:
                relay(p, s)

    def need(p):
        while any(q == p for q, _ in todo):
            pump(1)
        weights_done(p)

    scale2 = math.log2(math.e) / math.sqrt(HD)

    def attend(slot, first=False, base=0, steps=2, size=384):
        for i in range(steps):
            rows = pl.ds(pl.multiple_of(base + i * size, 64), size)
            s = lax.dot_general(
                qb[rows, :], kb[slot], (((1,), (1,)), ((), ())), preferred_element_type=F32
            )
            top = jnp.max(s, axis=1, keepdims=True)
            if not first:
                old = m_s[rows, :]
                top = jnp.maximum(top, old[:, :1])
            p = jnp.exp2((s - top) * scale2)
            part = p[:, 0:128]
            for t in range(1, 6):
                part = part + p[:, t * 128 : (t + 1) * 128]
            out = jnp.dot(p.astype(BF), vb[slot], preferred_element_type=F32)
            if not first:
                shrink = jnp.exp2((old - top) * scale2)
                part = part + l_s[rows, :] * shrink
                out = out + acc[rows, :] * shrink
            m_s[rows, :] = jnp.broadcast_to(top, (size, 128))
            l_s[rows, :] = part
            acc[rows, :] = out

    for d in own[0]:
        d.wait()
    begin(0)
    pass_half(0)
    pass_half(1)
    for p in range(len(slots)):
        if p:
            for d in own[p]:
                d.wait()
        x_send(p, 0, z)
    pump()
    lq.wait()
    lk.wait()
    lv.wait()
    arrived(qb.at[far_rows, :], qx_s.at[2], qx_r.at[2], pair)
    attend(z, first=True)
    def finish(rows, blocks):
        o = acc[rows, :] / jnp.sum(l_s[rows, :], axis=1, keepdims=True)
        ob[blocks] = o.astype(BF).reshape(8, ROWS, HD)

    far_blocks, own_blocks = pl.ds((1 - lo) * 8, 8), pl.ds(lo * 8, 8)
    for s in (1, 2, 3, 4):
        kv_relay(0, s)
        pump()
        if s > 1:
            attend(zmod(z + s - 1))
        kv_relay(1, s)
        relay(0, s)
        pump()
        if s < 4:
            attend(zmod(z - s))
    attend(zmod(z + 4), base=(1 - lo) * TOK, steps=2, size=192)
    finish(far_rows, far_blocks)
    send(ob.at[far_blocks], ho.at[:, :, own_cols], o_s, o_r, pair)
    pump()
    attend(zmod(z + 4), base=lo * TOK, steps=2, size=192)
    finish(own_rows, own_blocks)
    lo_copy = local(ob.at[own_blocks], ho.at[:, :, own_cols], 12)
    for i in range(3):
        for u in range(8):
            mrow[i : i + 1, u * 128 : (u + 1) * 128] = jnp.full((1, 128), mask_ref[i, u].astype(F32))
    lres.wait()
    stream[...] = res[...].astype(F32)
    lo_copy.wait()
    pump()
    arrived(ho.at[:, :, far_cols], o_s, o_r, pair)

    class Scatter:
        def __init__(self, part, out, got, ssem, rsem):
            self.part, self.out, self.got, self.ssem, self.rsem = part, out, got, ssem, rsem

        def put(self, i, value):
            self.out[i] = value.astype(BF)
            send(self.out.at[i], self.got.at[i], self.ssem.at[i], self.rsem.at[i], yl if i % 2 else yr)

        def take(self, i):
            arrived(self.got.at[i], self.ssem.at[i], self.rsem.at[i], yr if i % 2 else yl)
            return self.got[i].astype(F32)

        def first(self):
            right, left, far = ymod(y + 1), ymod(y - 1), ymod(y + 2)
            self.put(0, self.part(far, 0))
            self.put(1, self.part(far, 1))
            self.put(2, self.part(right, 1))
            self.put(3, self.part(left, 0))

        def direct(self):
            right, left, far = ymod(y + 1), ymod(y - 1), ymod(y + 2)
            for i, (b, to) in enumerate(((far, yo), (far, yo), (right, yr), (left, yl), (right, yr), (left, yl))):
                self.out[i] = self.part(b, (0, 1, 1, 0, 0, 1)[i]).astype(BF)
                send(self.out.at[i], self.got.at[i], self.ssem.at[i], self.rsem.at[i], to)

        def direct_total(self):
            halves = [self.part(y, 0), self.part(y, 1)]
            for i, frm in ((3, yr), (4, yl), (2, yl), (5, yr), (0, yo), (1, yo)):
                arrived(self.got.at[i], self.ssem.at[i], self.rsem.at[i], frm)
                halves[(0, 1, 1, 0, 0, 1)[i]] += self.got[i].astype(F32)
            return jnp.concatenate(halves, axis=1)

        def second(self):
            self.put(4, self.part(ymod(y + 1), 0) + self.take(0))
            self.put(5, self.part(ymod(y - 1), 1) + self.take(1))

        def total(self):
            low = self.part(y, 0) + self.take(3) + self.take(4)
            high = self.part(y, 1) + self.take(2) + self.take(5)
            return jnp.concatenate([low, high], axis=1)

    def branch(n, left, weight):
        for mine in (False, True):
            side = c if mine else 1 - c
            lhs = jnp.concatenate([left[2 * b + side] for b in range(NY)], axis=0)
            for j in range(4):
                cols = slice(j * 512, (j + 1) * 512)
                prod = jnp.dot(lhs, weight[:, cols], preferred_element_type=F32).reshape(NY, ROWS, 512)
                for r in range(CHUNKS):
                    chunk = prod[:, r * 16 : (r + 1) * 16]
                    if mine:
                        ps[r, :, :, cols] = chunk
                    else:
                        xs[n, r, :, :, cols] = chunk.astype(BF)
            if not mine:
                for r in range(CHUNKS):
                    send(xs.at[n, r], xr.at[n, r], pc_s.at[n, r], pc_r.at[n, r], core)
                pump()
        half = D // 2

        def part_of(r):
            def part(b, h):
                cols = slice(h * half, (h + 1) * half)
                return ps[r, b, :, cols] + xr[n, r, b, :, cols].astype(F32)

            return part

        chunks = [
            Scatter(part_of(r), rs.at[n, r], rr.at[n, r], rx_s.at[n, r], rx_r.at[n, r]) for r in range(CHUNKS)
        ]
        for r in range(CHUNKS):
            arrived(xr.at[n, r], pc_s.at[n, r], pc_r.at[n, r], core)
            if r:
                chunks[r].first()
            else:
                chunks[r].direct()
        for r in range(1, CHUNKS):
            pump()
            chunks[r].second()
        for r in range(CHUNKS):
            pump()
            rows = slice(r * 16, (r + 1) * 16)
            new = stream[rows, :] + (chunks[r].total() if r else chunks[r].direct_total())
            stream[rows, :] = new
            nb[n, mp, rows] = layer_norm(new).astype(BF)
            mine = nb.at[n, mp, rows]
            send(mine, mine, ag_s.at[n, r, 0], ag_r.at[n, r, 0], yr)
            send(mine, mine, ag_s.at[n, r, 1], ag_r.at[n, r, 1], yl)
            if r == CHUNKS - 1:
                send(mine, mine, ag_s.at[n, r, 2], ag_r.at[n, r, 2], yo)
            send(mine, mine, agc_s.at[n, r, 0], agc_r.at[n, r, 0], core)
        for r in range(CHUNKS):
            pump()
            rows = slice(r * 16, (r + 1) * 16)
            for i, (d, frm, to) in enumerate(((1, yl, yr), (3, yr, yl))):
                b = 2 * ymod(y - d) + c
                got, part = nb.at[n, b, rows], nb.at[n, b, rows, i * half : (i + 1) * half]
                arrived(got, ag_s.at[n, r, i], ag_r.at[n, r, i], frm)
                if r < CHUNKS - 1:
                    send(part, part, ag_s.at[n, r, 2 + i], ag_r.at[n, r, 2 + i], to)
                send(got, got, agc_s.at[n, r, d], agc_r.at[n, r, d], core)
        for r in range(CHUNKS):
            pump()
            rows = slice(r * 16, (r + 1) * 16)
            b = 2 * ymod(y + 2) + c
            if r < CHUNKS - 1:
                for i, frm in enumerate((yl, yr)):
                    part = nb.at[n, b, rows, i * half : (i + 1) * half]
                    arrived(part, ag_s.at[n, r, 2 + i], ag_r.at[n, r, 2 + i], frm)
            else:
                arrived(nb.at[n, b, rows], ag_s.at[n, r, 2], ag_r.at[n, r, 2], yo)
            send(nb.at[n, b, rows], nb.at[n, b, rows], agc_s.at[n, r, 2], agc_r.at[n, r, 2], core)
        for r in range(CHUNKS):
            rows = slice(r * 16, (r + 1) * 16)
            for d in (0, 1, 3, 2):
                arrived(nb.at[n, 2 * ymod(y - d) + 1 - c, rows], agc_s.at[n, r, d], agc_r.at[n, r, d], core)

    need(0)
    branch(0, ho, wo)

    need(1)

    def glu(rows):
        value = jnp.dot(rows, cv[:, 0:256], preferred_element_type=F32)
        gate = jnp.dot(rows, cv[:, 256:512], preferred_element_type=F32)
        return (value * jax.nn.sigmoid(gate)).astype(BF)

    edge = glu(jnp.concatenate([nb[0, 7, ROWS - 16 :, :], nb[0, 0, :16, :]], axis=0))
    gs[0] = edge[:16]
    gs[1] = edge[16:]
    send(gs.at[0], gr.at[0], h_s.at[0], h_r.at[0], after)
    send(gs.at[1], gr.at[1], h_s.at[1], h_r.at[1], before)
    gp[16 : 16 + TOK, :] = glu(nb[0].reshape(TOK, D)).astype(F32)
    pump()
    arrived(gr.at[0], h_s.at[0], h_r.at[0], before)
    arrived(gr.at[1], h_s.at[1], h_r.at[1], after)
    gp[0:16, :] = jnp.where(seq > 0, gr[0].astype(F32), 0.0)
    gp[16 + TOK :, :] = jnp.where(seq < 2 * NZ - 1, gr[1].astype(F32), 0.0)
    for r in range(8):
        sh[r] = gp[r + 1 : r + 1 + TOK + 24, :]

    def depth(i, carry):
        total = jnp.zeros((96, 256), F32)
        for t in range(TAPS):
            total = total + dk_ref[t : t + 1, :] * sh[t % 8, pl.ds(pl.multiple_of(i * 96 + t // 8 * 8, 8), 96), :]
        act[pl.ds(2 * i, 2)] = (total * jax.nn.sigmoid(total)).astype(BF).reshape(2, ROWS, 256)
        return carry

    lax.fori_loop(0, 4, depth, 0)
    pump()
    need(2)
    branch(1, act, co)

    need(3)
    need(4)

    def ffn(j, carry):
        cols = pl.ds(pl.multiple_of(j * 256, 256), 256)
        pre = jnp.dot(nb[1].reshape(TOK, D), fi[:, cols], preferred_element_type=F32)
        h = (pre * jax.nn.sigmoid(pre)).reshape(3, 128, 256) * mrow[:, cols][:, None, :]
        hid[:, :, cols] = h.astype(BF).reshape(8, ROWS, 256)
        return carry

    lax.fori_loop(0, 4, ffn, 0)
    def columns(g):
        return [
            pl.ds(pl.multiple_of((side * NZ + shard_of(k)) * 128, 128), 128)
            for side in (lo, 1 - lo) for k in (2 * g, 2 * g + 1)
        ]

    def part_of(g):
        return lambda b, h: ps3[g, b, :, h * 256 : (h + 1) * 256] + xr3[g, b, :, h * 256 : (h + 1) * 256].astype(F32)

    groups = [Scatter(part_of(g), rs3.at[g], rr3.at[g], rx3_s.at[g], rx3_r.at[g]) for g in range(GROUPS)]
    def open_group(g):
        arrived(xr3.at[g], pc3_s.at[g], pc3_r.at[g], core)
        groups[g].first()

    for g in range(GROUPS):
        while (5, g + 1) in todo or (6, g + 1) in todo:
            pump(1)
        for p in (5, 6):
            weights_done(p, (2 * g, 2 * g + 1))
        rhs = jnp.concatenate([fd[:, cols] for cols in columns(g)], axis=1)
        for mine in (False, True):
            side = c if mine else 1 - c
            lhs = jnp.concatenate([hid[2 * b + side] for b in range(NY)], axis=0)
            prod = jnp.dot(lhs, rhs, preferred_element_type=F32).reshape(NY, ROWS, 512)
            if mine:
                ps3[g] = prod
            else:
                xs3[g] = prod.astype(BF)
                send(xs3.at[g], xr3.at[g], pc3_s.at[g], pc3_r.at[g], core)
        if g:
            open_group(g - 1)
    arrived(xr3.at[GROUPS - 1], pc3_s.at[GROUPS - 1], pc3_r.at[GROUPS - 1], core)
    groups[GROUPS - 1].direct()
    for g in range(GROUPS - 1):
        groups[g].second()
    for g in range(GROUPS):
        total = groups[g].total() if g < GROUPS - 1 else groups[g].direct_total()
        for i, cols in enumerate(columns(g)):
            stream[:, cols] += 0.5 * total[:, i * 128 : (i + 1) * 128]
    out_ref[...] = layer_norm(stream[...])
    for d in pending:
        d.wait_send()


def on_device(*args):
    dma = pltpu.SemaphoreType.DMA
    any_spec = pl.BlockSpec(memory_space=pl.ANY)
    vmem, smem = pl.BlockSpec(memory_space=pltpu.VMEM), pl.BlockSpec(memory_space=pltpu.SMEM)
    v = pltpu.VMEM
    return pl.pallas_call(
        block_kernel,
        out_shape=jax.ShapeDtypeStruct((ROWS, D), F32),
        in_specs=[any_spec] * 7 + [vmem] + [any_spec] * 3 + [smem],
        out_specs=vmem,
        scratch_shapes=[
            v((2 * TOK, HD), BF), v((NZ, 2 * TOK, HD), BF), v((NZ, 2 * TOK, HD), BF),
            v((2 * TOK, 128), F32), v((2 * TOK, 128), F32), v((2 * TOK, HD), F32),
            v((16, ROWS, HD), BF), v((8, ROWS, 256), BF),
            v((256, D), BF), v((D, 512), BF), v((256, D), BF), v((D, 1024), BF), v((1024, D), BF),
            v((ROWS, D), BF), v((ROWS, D), F32), v((CHUNKS, NY, 16, D), F32),
            v((2, CHUNKS, NY, 16, D), BF), v((2, CHUNKS, NY, 16, D), BF),
            v((2, CHUNKS, 6, 16, D // 2), BF), v((2, CHUNKS, 6, 16, D // 2), BF),
            v((GROUPS, NY, ROWS, 512), F32), v((GROUPS, NY, ROWS, 512), BF), v((GROUPS, NY, ROWS, 512), BF),
            v((GROUPS, 6, ROWS, 256), BF), v((GROUPS, 6, ROWS, 256), BF),
            v((2, 8, ROWS, D), BF),
            v((TOK + 32, 256), F32), v((8, TOK + 24, 256), F32), v((2, 16, 256), BF), v((2, 16, 256), BF),
            v((8, ROWS, 256), BF), v((8, ROWS, 1024), BF), v((3, 1024), F32),
            dma((13,)), dma((3,)), dma((3,)), dma((2, 2, 2)), dma((2, 2, 2)), dma((2, 2, 3)), dma((2, 2, 3)),
            dma((7, 2, 4)), dma((7, 2, 4)), dma((7, 8)), dma((7, 8)), dma(()), dma(()),
            dma((2, CHUNKS)), dma((2, CHUNKS)), dma((2, CHUNKS, 6)), dma((2, CHUNKS, 6)),
            dma((2, CHUNKS, 4)), dma((2, CHUNKS, 4)), dma((2, CHUNKS, 4)), dma((2, CHUNKS, 4)),
            dma((GROUPS,)), dma((GROUPS,)), dma((GROUPS, 6)), dma((GROUPS, 6)),
            dma((2,)), dma((2,)),
        ],
        compiler_params=pltpu.CompilerParams(
            collective_id=0, has_side_effects=True, vmem_limit_bytes=60 * 1024 * 1024
        ),
        name="block",
    )(*args)


def solution(mesh):
    in_specs = (
        P(("dp", "seq"), None),
        P(("dp", "seq"), "mp"),
        P(("dp", "seq"), "mp"),
        P(("dp", "seq"), "mp"),
        P("mp", "seq"),
        P("seq", "mp"),
        P("seq", "mp"),
        P(None, "mp"),
        P("mp", "seq"),
        P("seq", "mp"),
        P("mp", "seq"),
        P(("dp", "seq"), "mp"),
    )
    out_specs = P(("dp", "seq", "mp"), None)
    return jax.shard_map(on_device, mesh=mesh, in_specs=in_specs, out_specs=out_specs, check_vma=False)
```
